128 devices in a mesh: src: 4 (over z_hi, core), rcv: 32 (over y, z_lo, x).
Axes of the slice: x: 4, y: 4, z: 4 (z_hi: 2, z_lo: 2; z = z_hi * 2 + z_lo), core: 2. Of those that a mesh axis runs over, the one named last changes fastest.
Arguments:
- traces: bfloat16 [4096, 16, 2000], P('rcv', 'src')
- src_index: int32 [256], P('src'), may hold values from 0 to 4095, as said below
- quality: int32 [4096, 16], P('rcv'), may hold values 0 or 1
Outputs:
- xcorr: float32 [256, 201, 4096], P('src', None, 'rcv')
The draws below stay inside these ranges and needn't reach their ends.
Inputs may be any that keep to these rules, and one draw needn't show every extreme that they name: `src_index`: the source numbered j within each group of 64 sources lies in receiver block j mod 32, among channels (j mod 32) * 128 up to that plus 128 - 1.
All inputs are finite; a program needn't handle non-finite values. No bound on the sum of `quality` on one device may be relied on, other than what follows from the above.
Results may differ from the reference program's by a relative error of at most 0.0067.
Values may be sent and summed in bfloat16 or wider, within the bound.
No kernel may reach another device: no remote copies, remote signals or barrier semaphores. Data moves between devices by JAX's collectives and lax.ppermute only.
A program may use at most 576 MiB of HBM per device.

```python
import math
import jax
import jax.numpy as jnp
from jax import lax

L = 2000
LAGH = 100
SEG = 16
SRC_DEV = 64
NSRC = 256
RCV_DEV = 128
BLOCKS = 32
CH = 4096


def draw_traces(key, part):
    key_base, key_scale = jax.random.split(key)
    shape = (CH, SEG, L)
    base = jax.random.normal(key_base, shape, jnp.float32)
    scale = jnp.exp(jax.random.uniform(key_scale, (CH, SEG, 1), jnp.float32, 0.0, math.log(10.0)))
    return (base * scale).astype(jnp.bfloat16)


def draw_src_index(key, part):
    number = jnp.arange(NSRC, dtype=jnp.int32)
    within = number % SRC_DEV
    block = within % BLOCKS
    position = jax.random.randint(key, (NSRC,), 0, RCV_DEV, dtype=jnp.int32)
    position = jnp.where(number == 0, 0, position)
    position = jnp.where(number == NSRC - 1, RCV_DEV - 1, position)
    return (block * RCV_DEV + position).astype(jnp.int32)


def touch_ends(result, rng, smallest, high):
    longest = result.shape.index(max(result.shape))
    spots = []
    for shift in (0, 1):
        where = [jax.random.randint(jax.random.fold_in(rng, axis), (), 0, length) for axis, length in enumerate(result.shape)]
        where[longest] = (where[longest] + shift) % result.shape[longest]
        spots.append(tuple(where))
    return result.at[spots[0]].set(smallest).at[spots[1]].set(high)


def setup_inputs(seed: int = 0) -> dict:
    arg_keys = jax.random.split(jax.random.key(seed), 4)
    return {
        "traces": draw_traces(jax.random.fold_in(arg_keys[3], 71), 0),
        "src_index": draw_src_index(jax.random.fold_in(arg_keys[3], 71), 0),
        "quality": touch_ends((jax.random.randint(arg_keys[2], (CH, SEG), 0, 4) < 3).astype(jnp.int32), jax.random.fold_in(arg_keys[2], 1), 0, 1),
    }


def make_tables():
    half = L // 2
    bins = jnp.arange(1, half + 1, dtype=jnp.int32)
    times = jnp.arange(L, dtype=jnp.int32)
    phase = (times[:, None] * bins[None, :] % L).astype(jnp.float32) * (2.0 * math.pi / L)
    forward = jnp.concatenate([jnp.cos(phase), -jnp.sin(phase)], axis=1).astype(jnp.bfloat16)
    lagvals = jnp.arange(-LAGH, LAGH + 1, dtype=jnp.int32)
    phase_lag = (bins[:, None] * lagvals[None, :] % L).astype(jnp.float32) * (2.0 * math.pi / L)
    weights = jnp.where(bins == half, 1.0, 2.0).astype(jnp.float32)[:, None] / jnp.sqrt(jnp.float32(half))
    inverse = jnp.concatenate([weights * jnp.cos(phase_lag), -weights * jnp.sin(phase_lag)], axis=0).astype(jnp.bfloat16)
    return (forward, inverse)

def whiten(samples, forward):
    half = L // 2
    flat = samples.reshape(-1, L)
    spec = jnp.dot(flat, forward, preferred_element_type=jnp.float32)
    real_part = spec[:, :half]
    imag_part = spec[:, half:]
    power = real_part * real_part + imag_part * imag_part
    level = 0.5 * jnp.sqrt(lax.optimization_barrier(jnp.mean(power, axis=1, keepdims=True)) + 1e-06)
    denom = jnp.maximum(jnp.sqrt(power), level)
    white = jnp.concatenate([real_part / denom, imag_part / denom], axis=1).astype(jnp.bfloat16)
    return white.reshape(samples.shape[0], samples.shape[1], L)

def reference(traces, src_index, quality):
    half = L // 2
    forward, inverse = make_tables()
    white = whiten(traces, forward)
    qf = quality.astype(jnp.float32)
    srcw = white[src_index]
    msrc = qf[src_index]
    count = jnp.dot(msrc, qf.T, preferred_element_type=jnp.float32)
    recv = white.astype(jnp.float32) * qf[:, :, None]
    recv_re = recv[:, :, :half]
    recv_im = recv[:, :, half:]
    inv32 = inverse.astype(jnp.float32)
    nblk = srcw.shape[0] // 4
    blocks_w = srcw.reshape(nblk, 4, srcw.shape[1], L)
    blocks_m = msrc.reshape(nblk, 4, msrc.shape[1])

    def one_block(pair):
        sw, ms = pair
        left = sw.astype(jnp.float32) * ms[:, :, None]
        left_re = left[:, :, :half]
        left_im = left[:, :, half:]
        pre = jnp.einsum('isk,jsk->ijk', left_re, recv_re) + jnp.einsum('isk,jsk->ijk', left_im, recv_im)
        pim = jnp.einsum('isk,jsk->ijk', left_im, recv_re) - jnp.einsum('isk,jsk->ijk', left_re, recv_im)
        cross = jnp.concatenate([pre, pim], axis=2).astype(jnp.bfloat16)
        return jnp.einsum('ijk,kt->itj', cross.astype(jnp.float32), inv32)
    lagged = lax.map(one_block, (blocks_w, blocks_m))
    lagged = lagged.reshape(srcw.shape[0], 2 * LAGH + 1, traces.shape[0])
    return lagged / jnp.maximum(count, 1.0)[:, None, :]
```

```python
import functools
import math

import jax
import jax.numpy as jnp
import ml_dtypes
import numpy as np
from jax import lax
from jax.experimental import pallas as pl
from jax.experimental.pallas import tpu as pltpu
from jax.sharding import Mesh, PartitionSpec as P

LAGH = 100
NLAG = 2 * LAGH + 1
TAU = 208
GRP = 8
KPAD = 1024
NGRP = KPAD // GRP
SDEV = 4
ROWS = 64
MB = 1 << 20


def start_tables(length):
    bins = np.arange(1, GRP + 1, dtype=np.float64)
    times = np.arange(length, dtype=np.float64)
    phase = 2.0 * math.pi / length * ((bins[:, None] * times[None, :]) % length)
    step = 2.0 * math.pi / length * ((GRP * times) % length)
    step = np.broadcast_to(step[None, :], phase.shape)
    return np.stack([np.cos(phase), -np.sin(phase), np.cos(step), np.sin(step)]).astype(np.float32)


def lag_table(half):
    bins = np.arange(1, half + 1, dtype=np.int64)
    lags = np.arange(-LAGH, LAGH + 1, dtype=np.int64)
    phase = 2.0 * math.pi / (2 * half) * ((lags[:, None] * bins[None, :]) % (2 * half))
    weight = np.where(bins == half, 1.0, 2.0)[None, :] / math.sqrt(half)
    out = np.zeros((TAU, 2, KPAD), np.float32)
    out[:NLAG, 0, :half] = weight * np.cos(phase)
    out[:NLAG, 1, :half] = -weight * np.sin(phase)
    return out.astype(ml_dtypes.bfloat16)


DBLK = 25


def spectra_kernel(half, x_ref, start_ref, qual_ref, y_ref, state, table, spec, power):
    ngrp = half // GRP
    state[0] = start_ref[0]
    state[1] = start_ref[1]
    power[...] = jnp.zeros_like(power)
    x01 = [x_ref[g] for g in range(4)]
    samples = jnp.concatenate(x01, axis=1)

    def gen(n, _):
        cos, sin = state[0], state[1]
        table[pl.ds(pl.multiple_of(n * 16, 16), 16), :] = jnp.concatenate([cos, sin], axis=0).astype(jnp.bfloat16)
        rc, rs = start_ref[2], start_ref[3]
        state[0] = cos * rc + sin * rs
        state[1] = sin * rc - cos * rs
        return 0

    def block(b, _):
        lax.fori_loop(0, DBLK, gen, 0)
        prod = jnp.dot(table[...], samples, preferred_element_type=jnp.float32)
        spec[pl.ds(pl.multiple_of(b * (DBLK * 16), DBLK * 16), DBLK * 16), :] = prod
        sq = prod * prod
        power[...] += jnp.sum(sq.reshape(DBLK * 2, 8, 512), axis=0)
        return 0

    lax.fori_loop(0, ngrp // DBLK, block, 0)
    mean = jnp.sum(power[...], axis=0, keepdims=True) * (1.0 / half)
    level2 = 0.25 * (mean + 1e-06)

    def white(n, _):
        base = pl.multiple_of(n * 16, 16)
        real = spec[pl.ds(base, 8), :]
        imag = spec[pl.ds(base + 8, 8), :]
        inv = lax.rsqrt(jnp.maximum(real * real + imag * imag, level2)) * qual_ref[...]
        parts = []
        for value in (real * inv, imag * inv):
            for g in range(4):
                parts.append(value[:, g * 128 : (g + 1) * 128])
        y_ref[pl.ds(pl.multiple_of(n * ROWS, ROWS), ROWS), :] = jnp.concatenate(parts, axis=0).astype(jnp.bfloat16)
        return 0

    lax.fori_loop(0, ngrp, white, 0)
    y_ref[pl.ds(ngrp * ROWS, (NGRP - ngrp) * ROWS), :] = jnp.zeros(((NGRP - ngrp) * ROWS, 128), jnp.bfloat16)


def spectra(samples, qual):
    length = samples.shape[1]
    half = length // 2
    start = jnp.asarray(start_tables(length))
    return pl.pallas_call(
        functools.partial(spectra_kernel, half),
        out_shape=jax.ShapeDtypeStruct((NGRP * ROWS, 128), jnp.bfloat16),
        scratch_shapes=[
            pltpu.VMEM((2, 8, length), jnp.float32),
            pltpu.VMEM((DBLK * 16, length), jnp.bfloat16),
            pltpu.VMEM((2 * half, 512), jnp.float32),
            pltpu.VMEM((8, 512), jnp.float32),
        ],
        compiler_params=pltpu.CompilerParams(vmem_limit_bytes=48 * MB),
        name="spectra",
    )(samples, start, qual)


CHUNKS = 4
CGRP = NGRP // CHUNKS
CK = KPAD // CHUNKS


def correlate_kernel(y_ref, x_ref, lag_ref, msrc_ref, qual_ref, out_ref, xrow, cross, acc):
    step = pl.program_id(0)
    rowid = lax.broadcasted_iota(jnp.int32, (16, 256), 0) % GRP
    lane = lax.broadcasted_iota(jnp.int32, (16, 256), 1) % GRP
    keep = rowid == lane
    zero = jnp.zeros((16, 256), jnp.bfloat16)

    def pair(n, _):
        halves = []
        for s in range(SDEV):
            halves.append(x_ref[:, s, pl.ds(pl.multiple_of(n * 128, 128), 128)].astype(jnp.float32))
        low = lax.broadcasted_iota(jnp.int32, (64, 128), 1) < 64
        prods = []
        for a in range(2):
            cols = []
            for q in range(2):
                left, right = halves[2 * q], halves[2 * q + 1]
                if a == 0:
                    cols.append(jnp.where(low, left, pltpu.roll(right, 64, 1)))
                else:
                    cols.append(jnp.where(low, pltpu.roll(left, 64, 1), right))
            xrow[a] = jnp.concatenate(cols, axis=1)
            tiles = []
            for i in range(0, 64, 2):
                two = jnp.concatenate(
                    [xrow[a, pl.ds(i, 8, stride=0), :], xrow[a, pl.ds(i + 1, 8, stride=0), :]], axis=0
                ).astype(jnp.bfloat16)
                tiles.append(jnp.where(keep, two, zero))
            lhs = jnp.concatenate(tiles, axis=0)
            base = pl.multiple_of((2 * n + a) * ROWS, ROWS)
            reim, imre = [], []
            for s in range(SDEV):
                yr = y_ref[s, pl.ds(base, 32), :]
                yi = y_ref[s, pl.ds(base + 32, 32), :]
                reim += [yr, yi]
                imre += [-yi, yr]
            right = jnp.concatenate(
                [jnp.concatenate(reim, axis=0), jnp.concatenate(imre, axis=0)], axis=1
            )
            prods.append(jnp.dot(lhs, right, preferred_element_type=jnp.float32))
        off = pl.multiple_of(n * 16, 16)
        for i in range(64):
            both = jnp.concatenate([prods[0][8 * i : 8 * i + 8], prods[1][8 * i : 8 * i + 8]], axis=0).astype(
                jnp.bfloat16
            )
            cross[i, pl.ds(off, 16), :] = both[:, :128]
            cross[i, pl.ds(pl.multiple_of(CK + off, 16), 16), :] = both[:, 128:]
        return 0

    lax.fori_loop(0, CGRP // 2, pair, 0)

    @pl.when(step == 0)
    def _():
        acc[...] = jnp.zeros_like(acc)

    table = lag_ref[0]

    def lags(n, _):
        right = jnp.concatenate([cross[2 * n], cross[2 * n + 1]], axis=1)
        prod = jnp.dot(table, right, preferred_element_type=jnp.float32)
        acc[2 * n] += prod[:, :128]
        acc[2 * n + 1] += prod[:, 128:]
        return 0

    lax.fori_loop(0, 32, lags, 0)

    @pl.when(step == CHUNKS - 1)
    def _():
        count = jnp.dot(msrc_ref[...], qual_ref[...], preferred_element_type=jnp.float32)
        xrow[0, :, :128] = 1.0 / jnp.maximum(count, 1.0)

        def source(p):
            return (p % 2) * 32 + (p // 16) * 8 + (p // 2) % 2 * 4 + (p // 4) % 4

        def finish(t, _):
            for p in range(64):
                scale = xrow[0, pl.ds(p, 8, stride=0), :128]
                lagged = acc[p, pl.ds(pl.multiple_of(t * 8, 8), 8), :]
                out_ref[pl.ds(t * 512 + source(p), 8, stride=64), :] = lagged * scale
            return 0

        lax.fori_loop(0, NLAG // 8, finish, 0)
        for p in range(64):
            out_ref[pl.ds((NLAG - 1) * 64 + source(p), 1), :] = (
                acc[p, NLAG - 1 : NLAG, :] * xrow[0, p : p + 1, :128]
            )


def correlate(y_all, x_all, msrc, qual_t):
    table = lag_table(1000)
    table = table.reshape(TAU, 2, CHUNKS, CK).transpose(2, 0, 1, 3).reshape(CHUNKS, TAU, 2 * CK)
    return pl.pallas_call(
        correlate_kernel,
        grid=(CHUNKS,),
        out_shape=jax.ShapeDtypeStruct((NLAG * 64, 128), jnp.float32),
        in_specs=[
            pl.BlockSpec((SDEV, CGRP * ROWS, 128), lambda c: (0, c, 0)),
            pl.BlockSpec((64, SDEV, CGRP * ROWS), lambda c: (0, 0, c)),
            pl.BlockSpec((1, TAU, 2 * CK), lambda c: (c, 0, 0)),
            pl.BlockSpec((64, 16), lambda c: (0, 0)),
            pl.BlockSpec((16, 128), lambda c: (0, 0)),
        ],
        out_specs=pl.BlockSpec((NLAG * 64, 128), lambda c: (0, 0)),
        scratch_shapes=[
            pltpu.VMEM((2, 64, 256), jnp.float32),
            pltpu.VMEM((64, 2 * CK, 128), jnp.bfloat16),
            pltpu.VMEM((64, TAU, 128), jnp.float32),
        ],
        compiler_params=pltpu.CompilerParams(vmem_limit_bytes=60 * MB),
        name="correlate",
    )(y_all, x_all, jnp.asarray(table), msrc, qual_t)


def on_device(traces, src_index, quality):
    rows = traces.shape[0]
    samples = jnp.transpose(traces, (1, 2, 0))
    qual_t = jnp.transpose(quality, (1, 0))
    me = lax.axis_index(("zhi", "core"))
    first = lax.axis_index(("y", "zlo", "x")) * rows
    r = lax.axis_index(("y", "zlo", "x"))
    qual_f = qual_t.astype(jnp.float32)
    qual_own = lax.dynamic_slice_in_dim(qual_f, me * 4, 4, axis=0).reshape(1, 512)
    y = spectra(samples, qual_own)
    index_all = lax.all_gather(src_index, ("zhi", "core"), axis=0, tiled=False)
    mine = index_all.reshape(4, 2, 32)
    mine = lax.dynamic_slice_in_dim(mine, r, 1, axis=2).reshape(8)
    onehot = (mine[:, None] == first + jnp.arange(rows, dtype=jnp.int32)[None, :]).astype(jnp.bfloat16)
    sel = lax.dot_general(onehot, y, (((1,), (1,)), ((), ())), preferred_element_type=jnp.float32)
    sel = sel.astype(jnp.bfloat16).reshape(4, 2, NGRP * ROWS)
    got = lax.all_to_all(sel, ("zhi", "core"), 0, 0, tiled=False)
    own = lax.dynamic_slice_in_dim(onehot, me * 2, 2, axis=0)
    msel = jnp.dot(own, qual_f.astype(jnp.bfloat16).T, preferred_element_type=jnp.float32).astype(jnp.bfloat16)
    payload = jnp.concatenate(
        [jnp.transpose(got, (1, 0, 2)).reshape(2, -1), jnp.pad(msel, ((0, 0), (0, 112)))], axis=1
    )
    payload = lax.all_gather(payload, "zlo", axis=0, tiled=True)
    payload = lax.all_gather(payload, ("y", "x"), axis=0, tiled=True)
    x_all = payload[:, : 4 * NGRP * ROWS].reshape(64, 4, NGRP * ROWS)
    msrc = payload[:, 4 * NGRP * ROWS : 4 * NGRP * ROWS + 16]
    y_all = lax.all_gather(y, ("zhi", "core"), axis=0, tiled=False)
    out = correlate(y_all, x_all, msrc, qual_f.astype(jnp.bfloat16))
    return jnp.transpose(out.reshape(NLAG, 64, 128), (1, 0, 2))


def solution(mesh):
    fine = Mesh(mesh.devices.reshape(2, 2, 4, 2, 4), ("zhi", "core", "y", "zlo", "x"))
    rcv = ("y", "zlo", "x")
    src = ("zhi", "core")
    return jax.shard_map(
        on_device,
        mesh=fine,
        in_specs=(P(rcv, src, None), P(src), P(rcv, None)),
        out_specs=P(src, None, rcv),
        check_vma=False,
    )
```

```python
import functools
import math

import jax
import jax.numpy as jnp
import ml_dtypes
import numpy as np
from jax import lax
from jax.experimental import pallas as pl
from jax.experimental.pallas import tpu as pltpu
from jax.sharding import Mesh, PartitionSpec as P

LAGH = 100
NLAG = 2 * LAGH + 1
TAU = 208
GRP = 8
KPAD = 1024
NGRP = KPAD // GRP
SDEV = 4
ROWS = 64
MB = 1 << 20


def start_tables(length):
    bins = np.arange(1, GRP + 1, dtype=np.float64)
    times = np.arange(length, dtype=np.float64)
    phase = 2.0 * math.pi / length * ((bins[:, None] * times[None, :]) % length)
    step = 2.0 * math.pi / length * ((GRP * times) % length)
    step = np.broadcast_to(step[None, :], phase.shape)
    return np.stack([np.cos(phase), -np.sin(phase), np.cos(step), np.sin(step)]).astype(np.float32)


def lag_table(half):
    bins = np.arange(1, half + 1, dtype=np.int64)
    lags = np.arange(-LAGH, LAGH + 1, dtype=np.int64)
    phase = 2.0 * math.pi / (2 * half) * ((lags[:, None] * bins[None, :]) % (2 * half))
    weight = np.where(bins == half, 1.0, 2.0)[None, :] / math.sqrt(half)
    out = np.zeros((TAU, 2, KPAD), np.float32)
    out[:NLAG, 0, :half] = weight * np.cos(phase)
    out[:NLAG, 1, :half] = -weight * np.sin(phase)
    return out.astype(ml_dtypes.bfloat16)


DBLK = 25


def spectra_kernel(half, x_ref, start_ref, qual_ref, flag_ref, hot_ref, y0_ref, y1_ref, sel_ref, y_ref, state, table, spec, power):
    ngrp = half // GRP
    state[0] = start_ref[0]
    state[1] = start_ref[1]
    power[...] = jnp.zeros_like(power)
    x01 = [x_ref[g] for g in range(4)]
    samples = jnp.concatenate(x01, axis=1)

    def gen(n, _):
        cos, sin = state[0], state[1]
        table[pl.ds(pl.multiple_of(n * 16, 16), 16), :] = jnp.concatenate([cos, sin], axis=0).astype(jnp.bfloat16)
        rc, rs = start_ref[2], start_ref[3]
        state[0] = cos * rc + sin * rs
        state[1] = sin * rc - cos * rs
        return 0

    def block(b, _):
        lax.fori_loop(0, DBLK, gen, 0)
        prod = jnp.dot(table[...], samples, preferred_element_type=jnp.float32)
        spec[pl.ds(pl.multiple_of(b * (DBLK * 16), DBLK * 16), DBLK * 16), :] = prod
        sq = prod * prod
        power[...] += jnp.sum(sq.reshape(DBLK * 2, 8, 512), axis=0)
        return 0

    lax.fori_loop(0, ngrp // DBLK, block, 0)
    mean = jnp.sum(power[...], axis=0, keepdims=True) * (1.0 / half)
    level2 = 0.25 * (mean + 1e-06)

    def white(n, _):
        base = pl.multiple_of(n * 16, 16)
        real = spec[pl.ds(base, 8), :]
        imag = spec[pl.ds(base + 8, 8), :]
        inv = lax.rsqrt(jnp.maximum(real * real + imag * imag, level2)) * qual_ref[...]
        parts = []
        for value in (real * inv, imag * inv):
            for g in range(4):
                parts.append(value[:, g * 128 : (g + 1) * 128])
        y_ref[pl.ds(pl.multiple_of(n * ROWS, ROWS), ROWS), :] = jnp.concatenate(parts, axis=0).astype(jnp.bfloat16)
        return 0

    lax.fori_loop(0, ngrp, white, 0)
    y_ref[pl.ds(ngrp * ROWS, (NGRP - ngrp) * ROWS), :] = jnp.zeros(((NGRP - ngrp) * ROWS, 128), jnp.bfloat16)
    y_ref[pl.ds((NGRP - 1) * ROWS, 16), :] = flag_ref[...].astype(jnp.bfloat16)
    y0_ref[...] = y_ref[: CHUNKS[0] * 8, :]
    y1_ref[...] = y_ref[CHUNKS[0] * 8 :, :]
    picked = lax.dot_general(
        hot_ref[...], y_ref[...], (((1,), (1,)), ((), ())), preferred_element_type=jnp.float32
    )
    sel_ref[...] = picked.astype(jnp.bfloat16)


def spectra(samples, qual, flags, onehot):
    length = samples.shape[1]
    half = length // 2
    start = jnp.asarray(start_tables(length))
    return pl.pallas_call(
        functools.partial(spectra_kernel, half),
        out_shape=[
            jax.ShapeDtypeStruct((CHUNKS[0] * 8, 128), jnp.bfloat16),
            jax.ShapeDtypeStruct((CHUNKS[1] * 8, 128), jnp.bfloat16),
            jax.ShapeDtypeStruct((8, NGRP * ROWS), jnp.bfloat16),
        ],
        scratch_shapes=[
            pltpu.VMEM((NGRP * ROWS, 128), jnp.bfloat16),
            pltpu.VMEM((2, 8, length), jnp.float32),
            pltpu.VMEM((DBLK * 16, length), jnp.bfloat16),
            pltpu.VMEM((2 * half, 512), jnp.float32),
            pltpu.VMEM((8, 512), jnp.float32),
        ],
        compiler_params=pltpu.CompilerParams(vmem_limit_bytes=48 * MB),
        name="spectra",
    )(samples, start, qual, flags, onehot)


UNROLL = 4
CHUNKS = (640, 384)


def correlate_kernel(first, last, kc, *refs):
    where_ref, seg_ref, ya, yb, yc, yd, xa, xb, xc, xd, lag_ref, qual_ref = refs[:12]
    if first:
        out_ref, ybuf, xbuf, xrow, cross, sems = refs[12:]
        acc_ref = None
    else:
        acc_hbm, out_ref, ybuf, xbuf, xrow, cross, sems, acc_ref, scale, stage, osem = refs[12:]
    copies = []
    for j, ref in enumerate((ya, yb, yc, yd)):
        copies.append(pltpu.make_async_copy(ref, ybuf.at[seg_ref[j]], sems.at[j]))
    for j, ref in enumerate((xa, xb, xc, xd)):
        copies.append(pltpu.make_async_copy(ref, xbuf.at[j], sems.at[4 + j]))
    for copy in copies:
        copy.start()
    if not first:
        prefetch = pltpu.make_async_copy(acc_hbm, acc_ref, sems.at[8])
        prefetch.start()
    for copy in copies:
        copy.wait()

    rowid = lax.broadcasted_iota(jnp.int32, (16, 256), 0) % GRP
    lane = lax.broadcasted_iota(jnp.int32, (16, 256), 1) % GRP
    keep = rowid == lane
    zero = jnp.zeros((16, 256), jnp.bfloat16)
    stay = (lax.broadcasted_iota(jnp.int32, (8, 128), 0) < 4) == (lax.broadcasted_iota(jnp.int32, (8, 128), 1) < 64)

    def pair(n, slot):
        for far in range(4):
            for near in range(4):
                tile = xbuf[far, near * 16 : near * 16 + 16, pl.ds(pl.multiple_of(n * 128, 128), 128)].astype(jnp.float32)
                for half in range(2):
                    part = tile[half * 8 : half * 8 + 8]
                    moved = pltpu.roll(pltpu.roll(part, 4, 0), 64, 1)
                    row = (far * 4 + near) * 8
                    xrow[slot, row : row + 8, half * 128 : half * 128 + 128] = jnp.where(stay, part, moved)
        prods = []
        for a in range(2):
            tiles = []
            for p in range(0, 64, 2):
                row = (p // 4) * 8 + a * 4 + p % 4
                two = jnp.concatenate(
                    [xrow[slot, pl.ds(row, 8, stride=0), :], xrow[slot, pl.ds(row + 1, 8, stride=0), :]], axis=0
                ).astype(jnp.bfloat16)
                tiles.append(jnp.where(keep, two, zero))
            lhs = jnp.concatenate(tiles, axis=0)
            base = pl.multiple_of((2 * n + a) * ROWS, ROWS)
            reim, imre = [], []
            for s in range(SDEV):
                yr = ybuf[s, pl.ds(base, 32), :]
                yi = ybuf[s, pl.ds(base + 32, 32), :]
                reim += [yr, yi]
                imre += [-yi, yr]
            right = jnp.concatenate([jnp.concatenate(reim, axis=0), jnp.concatenate(imre, axis=0)], axis=1)
            prods.append(jnp.dot(lhs, right, preferred_element_type=jnp.float32))
        off = pl.multiple_of(n * 16, 16)
        for p in range(64):
            both = jnp.concatenate([prods[0][8 * p : 8 * p + 8], prods[1][8 * p : 8 * p + 8]], axis=0)
            both = both.astype(jnp.bfloat16)
            cross[p, pl.ds(off, 16), :] = both[:, :128]
            cross[p, pl.ds(pl.multiple_of(kc + off, 16), 16), :] = both[:, 128:]

    def pairs(m, _):
        for v in range(UNROLL):
            pair(m * UNROLL + v, v)
        return 0

    lax.fori_loop(0, kc // 16 // UNROLL, pairs, 0)
    table = lag_ref[...]
    if last:
        flags = []
        for far in range(4):
            for near in range(4):
                flags.append(xbuf[far, near * 16 : near * 16 + 4, kc * 8 - 128 :])
        flags = jnp.concatenate([f.astype(jnp.float32) for f in flags], axis=0)[:, 64:80].astype(jnp.bfloat16)
        count = jnp.dot(flags, qual_ref[...], preferred_element_type=jnp.float32)
        scale[...] = 1.0 / jnp.maximum(count, 1.0)
        prefetch.wait()

    def flush(n, slot):
        return pltpu.make_async_copy(stage.at[slot], out_ref.at[:, pl.ds(pl.multiple_of(n * 8, 8), 8), :], osem.at[slot])

    def lags(n, _):
        spots = [where_ref[n * 8 + j] for j in range(8)]
        parts = []
        for q in range(4):
            right = jnp.concatenate([cross[spots[2 * q]], cross[spots[2 * q + 1]]], axis=1)
            prod = jnp.dot(table, right, preferred_element_type=jnp.float32)
            parts += [prod[:, :128], prod[:, 128:]]
        if last:
            slot = n % 2
            parts = [(part + acc_ref[p]) * scale[pl.ds(p, 1), :] for part, p in zip(parts, spots)]

            @pl.when(n >= 2)
            def _():
                flush(n - 2, slot).wait()

            stage[slot] = pltpu.einshape("itj->tij", jnp.stack(parts, axis=0))[:NLAG]
            flush(n, slot).start()
        else:
            for part, p in zip(parts, spots):
                out_ref[p] = part
        return 0

    lax.fori_loop(0, 8, lags, 0)
    if last:
        flush(6, 0).wait()
        flush(7, 1).wait()


def correlate(first, last, kc, where, seg, ys, xs, table, qual_t, acc=None):
    smem = pl.BlockSpec(memory_space=pltpu.SMEM)
    hbm = pl.BlockSpec(memory_space=pl.ANY)
    vmem = pl.BlockSpec(memory_space=pltpu.VMEM)
    args = (where, seg, *ys, *xs, table, qual_t)
    in_specs = [smem, smem] + [hbm] * 8 + [vmem, vmem]
    scratch = [
        pltpu.VMEM((4, kc * 8, 128), jnp.bfloat16),
        pltpu.VMEM((4, 64, kc * 8), jnp.bfloat16),
        pltpu.VMEM((UNROLL, 128, 256), jnp.float32),
        pltpu.VMEM((64, 2 * kc, 128), jnp.bfloat16),
        pltpu.SemaphoreType.DMA((9,)),
    ]
    if first:
        out_shape, out_specs = (64, TAU, 128), vmem
    else:
        out_shape, out_specs = (NLAG, 64, 128), hbm
        args += (acc,)
        in_specs += [hbm]
        scratch += [
            pltpu.VMEM((64, TAU, 128), jnp.float32),
            pltpu.VMEM((64, 128), jnp.float32),
            pltpu.VMEM((2, NLAG, 8, 128), jnp.float32),
            pltpu.SemaphoreType.DMA((2,)),
        ]
    return pl.pallas_call(
        functools.partial(correlate_kernel, first, last, kc),
        out_shape=jax.ShapeDtypeStruct(out_shape, jnp.float32),
        in_specs=in_specs,
        out_specs=out_specs,
        scratch_shapes=scratch,
        compiler_params=pltpu.CompilerParams(vmem_limit_bytes=60 * MB),
        name="correlate_first" if first else "correlate_last",
    )(*args)


AXES = ("zhi", "core", "y", "zlo", "x")
SIZES = (2, 2, 4, 2, 4)


def permutation(move):
    out = []
    for flat in range(128):
        at = list(np.unravel_index(flat, SIZES))
        to = move(*[int(v) for v in at])
        out.append((flat, int(np.ravel_multi_index([v % n for v, n in zip(to, SIZES)], SIZES))))
    return out


def send(value, move):
    return lax.ppermute(value, AXES, permutation(move))


def sibling(zhi, core, y, zlo, x):
    return zhi, core + 1, y, zlo, x


def across(zhi, core, y, zlo, x):
    return zhi + 1, core, y, zlo, x


def ring(phase, d):
    def move(zhi, core, y, zlo, x):
        if core == phase:
            return zhi, core, y, zlo, x + d
        return zhi, core, y + d, zlo, x

    return move


def on_device(traces, src_index, quality):
    rows = traces.shape[0]
    samples = jnp.transpose(traces, (1, 2, 0))
    qual_f = jnp.transpose(quality, (1, 0)).astype(jnp.float32)
    zhi, core, yy, zlo, xx = [lax.axis_index(a) for a in AXES]
    me = zhi * 2 + core
    r = yy * 8 + zlo * 4 + xx
    qual_own = lax.dynamic_slice_in_dim(qual_f, me * 4, 4, axis=0).reshape(1, 512)
    index_all = lax.all_gather(src_index, ("zhi", "core"), axis=0, tiled=False)
    mine = lax.dynamic_slice_in_dim(index_all.reshape(4, 2, 32), r, 1, axis=2).reshape(8) - r * rows
    onehot = (mine[:, None] == jnp.arange(rows, dtype=jnp.int32)[None, :]).astype(jnp.bfloat16)
    table = lag_table(1000)
    tables, start = [], 0
    for kc in CHUNKS:
        tables.append(jnp.asarray(np.ascontiguousarray(table[:, :, start : start + kc]).reshape(TAU, 2 * kc)))
        start += kc

    y0, y1, sel = spectra(samples, qual_own, qual_f, onehot)
    ys0 = [y0]
    ys1 = [y1]
    far0 = send(y0, across)
    far1 = send(y1, across)
    near0, near1 = send(y0, sibling), send(y1, sibling)

    sel = sel.reshape(4, 1, 2, -1)
    slots = jnp.broadcast_to(sel, (4, 2, 2, sel.shape[-1])).reshape(8, 2, -1)
    got = lax.all_to_all(slots, ("zhi", "core", "zlo"), 0, 0, tiled=False)
    got = got.reshape(16, -1)
    xs = []
    start = 0
    for kc in CHUNKS:
        own = got[:, start * 8 : (start + kc) * 8]
        start += kc
        line = jnp.concatenate([own] + [send(own, ring(0, d)) for d in (1, 2, 3)], axis=0)
        xs.append([line] + [send(line, ring(1, d)) for d in (1, 2, 3)])

    i = jnp.arange(64, dtype=jnp.int32)
    dx, dy = (xx - i % 4) % 4, (yy - (i // 8) % 4) % 4
    far_step, near_step = jnp.where(core == 0, dy, dx), jnp.where(core == 0, dx, dy)
    where = far_step * 16 + near_step * 4 + (i // 4) % 2 * 2 + i // 32
    seg = jnp.bitwise_xor(me, jnp.arange(4, dtype=jnp.int32))
    qual_b = qual_f.astype(jnp.bfloat16)
    acc = correlate(
        True, False, CHUNKS[0], where, seg, (y0, near0, far0, send(far0, sibling)), xs[0], tables[0], qual_b
    )
    out = correlate(
        False, True, CHUNKS[1], where, seg, (y1, near1, far1, send(far1, sibling)), xs[1], tables[1], qual_b, acc
    )
    return jnp.transpose(out, (1, 0, 2))


def solution(mesh):
    fine = Mesh(mesh.devices.reshape(2, 2, 4, 2, 4), ("zhi", "core", "y", "zlo", "x"))
    rcv = ("y", "zlo", "x")
    src = ("zhi", "core")
    return jax.shard_map(
        on_device,
        mesh=fine,
        in_specs=(P(rcv, src, None), P(src), P(rcv, None)),
        out_specs=P(src, None, rcv),
        check_vma=False,
    )
```

```python
import functools
import math

import jax
import jax.numpy as jnp
import ml_dtypes
import numpy as np
from jax import lax
from jax.experimental import pallas as pl
from jax.experimental.pallas import tpu as pltpu
from jax.sharding import Mesh, PartitionSpec as P

LAGH = 100
NLAG = 2 * LAGH + 1
TAU = 208
GRP = 8
KPAD = 1024
NGRP = KPAD // GRP
SDEV = 4
ROWS = 64
MB = 1 << 20


def start_tables(length):
    bins = np.arange(1, GRP + 1, dtype=np.float64)
    times = np.arange(length, dtype=np.float64)
    phase = 2.0 * math.pi / length * ((bins[:, None] * times[None, :]) % length)
    step = 2.0 * math.pi / length * ((GRP * times) % length)
    step = np.broadcast_to(step[None, :], phase.shape)
    return np.stack([np.cos(phase), -np.sin(phase), np.cos(step), np.sin(step)]).astype(np.float32)


def lag_table(half):
    bins = np.arange(1, half + 1, dtype=np.int64)
    lags = np.arange(-LAGH, LAGH + 1, dtype=np.int64)
    phase = 2.0 * math.pi / (2 * half) * ((lags[:, None] * bins[None, :]) % (2 * half))
    weight = np.where(bins == half, 1.0, 2.0)[None, :] / math.sqrt(half)
    out = np.zeros((TAU, 2, KPAD), np.float32)
    out[:NLAG, 0, :half] = weight * np.cos(phase)
    out[:NLAG, 1, :half] = -weight * np.sin(phase)
    return out.astype(ml_dtypes.bfloat16)


def cost(us):
    return pl.CostEstimate(flops=int(us * 1.1e9), transcendentals=0, bytes_accessed=1 << 20)


DBLK = 25
CHUNKS = (576, 448)


def spectra_kernel(half, me_ref, x_hbm, start_ref, qual_ref, y0_ref, y1_ref, y_ref, x_ref, state, table, spec, power, sem):
    ngrp = half // GRP
    length = 2 * half
    blocks = ngrp // DBLK
    load = pltpu.make_async_copy(x_hbm, x_ref, sem)
    load.start()

    def gen(slot):
        for lo in range(0, length, 128):
            cols = slice(lo, min(lo + 128, length))
            cos, sin = state[0, :, cols], state[1, :, cols]
            rc, rs = start_ref[2, :, cols], start_ref[3, :, cols]
            for n in range(DBLK):
                table[slot, n * 16 : n * 16 + 16, cols] = jnp.concatenate([cos, sin], axis=0).astype(jnp.bfloat16)
                cos, sin = cos * rc + sin * rs, sin * rc - cos * rs
            state[0, :, cols] = cos
            state[1, :, cols] = sin

    state[0] = start_ref[0]
    state[1] = start_ref[1]
    power[...] = jnp.zeros_like(power)
    gen(0)
    load.wait()
    samples = jnp.concatenate([x_ref[g] for g in range(4)], axis=1)

    def block(b, _):
        slot = b % 2
        prod = jnp.dot(table[slot], samples, preferred_element_type=jnp.float32)
        gen(1 - slot)
        spec[pl.ds(pl.multiple_of(b * (DBLK * 16), DBLK * 16), DBLK * 16), :] = prod
        power[...] += jnp.sum((prod * prod).reshape(DBLK * 2, 8, 512), axis=0)
        return 0

    lax.fori_loop(0, blocks, block, 0)
    mean = jnp.sum(power[...], axis=0, keepdims=True) * (1.0 / half)
    level2 = 0.25 * (mean + 1e-06)
    own = [qual_ref[pl.ds(me_ref[0] * 4 + g, 1), :].astype(jnp.float32) for g in range(4)]

    def whiten(n, part_ref, m):
        base = pl.multiple_of(n * 16, 16)
        reals, imags = [], []
        for g in range(4):
            cols = slice(g * 128, (g + 1) * 128)
            real = spec[pl.ds(base, 8), cols]
            imag = spec[pl.ds(base + 8, 8), cols]
            inv = lax.rsqrt(jnp.maximum(real * real + imag * imag, level2[:, cols])) * own[g]
            reals.append(real * inv)
            imags.append(imag * inv)
        value = jnp.concatenate(reals + imags, axis=0).astype(jnp.bfloat16)
        part_ref[pl.ds(pl.multiple_of(m * ROWS, ROWS), ROWS), :] = value
        y_ref[pl.ds(pl.multiple_of(n * ROWS, ROWS), ROWS), :] = value

    first = CHUNKS[0] // GRP

    def sweep(lo, hi, part_ref):
        def some(m, _):
            for v in range(4):
                whiten(lo + m * 4 + v, part_ref, m * 4 + v)
            return 0

        lax.fori_loop(0, (hi - lo) // 4, some, 0)
        for n in range(hi - (hi - lo) % 4, hi):
            whiten(n, part_ref, n - lo)

    sweep(0, first, y0_ref)
    sweep(first, ngrp, y1_ref)
    tail = (ngrp - first) * ROWS
    for ref in (y1_ref, y_ref):
        rows = ref.shape[0]
        ref[rows - CHUNKS[1] * 8 + tail :, :] = jnp.zeros((CHUNKS[1] * 8 - tail, 128), jnp.bfloat16)
        ref[rows - ROWS : rows - ROWS + 16, :] = qual_ref[...].astype(jnp.float32).astype(jnp.bfloat16)


def spectra(samples, qual_t, me):
    length = samples.shape[1]
    half = length // 2
    start = jnp.asarray(start_tables(length))
    vmem = pl.BlockSpec(memory_space=pltpu.VMEM)
    return pl.pallas_call(
        functools.partial(spectra_kernel, half),
        out_shape=[
            jax.ShapeDtypeStruct((CHUNKS[0] * 8, 128), jnp.bfloat16),
            jax.ShapeDtypeStruct((CHUNKS[1] * 8, 128), jnp.bfloat16),
            jax.ShapeDtypeStruct((NGRP * ROWS, 128), jnp.bfloat16),
        ],
        in_specs=[pl.BlockSpec(memory_space=pltpu.SMEM), pl.BlockSpec(memory_space=pl.ANY), vmem, vmem],
        out_specs=[vmem, vmem, vmem],
        scratch_shapes=[
            pltpu.VMEM((4, length, 128), jnp.bfloat16),
            pltpu.VMEM((2, 8, length), jnp.float32),
            pltpu.VMEM((2, DBLK * 16, length), jnp.bfloat16),
            pltpu.VMEM((2 * half, 512), jnp.float32),
            pltpu.VMEM((8, 512), jnp.float32),
            pltpu.SemaphoreType.DMA,
        ],
        compiler_params=pltpu.CompilerParams(vmem_limit_bytes=48 * MB),
        cost_estimate=cost(10),
        name="spectra",
    )(me, samples, start, qual_t)


def select_kernel(me_ref, ia, ib, ic, id_, y_ref, out_ref):
    me, r = me_ref[0], me_ref[1]
    row = lax.broadcasted_iota(jnp.int32, (16, 128), 0)
    lane = lax.broadcasted_iota(jnp.int32, (16, 128), 1)
    hot = jnp.zeros((16, 128), jnp.float32)
    for rel, ref in enumerate((ia, ib, ic, id_)):
        group = jnp.bitwise_xor(me, rel)
        for h in range(2):
            here = (row // 4 == group) & (row % 2 == h) & (lane == ref[r + 32 * h] - r * 128)
            hot = jnp.where(here, 1.0, hot)
    hot = hot.astype(jnp.bfloat16)
    picked = lax.dot_general(hot, y_ref[...], (((1,), (1,)), ((), ())), preferred_element_type=jnp.float32)
    out_ref[...] = picked.astype(jnp.bfloat16)


def select(where, lists, y):
    smem = pl.BlockSpec(memory_space=pltpu.SMEM)
    vmem = pl.BlockSpec(memory_space=pltpu.VMEM)
    return pl.pallas_call(
        select_kernel,
        out_shape=jax.ShapeDtypeStruct((16, NGRP * ROWS), jnp.bfloat16),
        in_specs=[smem] * 5 + [vmem],
        out_specs=vmem,
        compiler_params=pltpu.CompilerParams(vmem_limit_bytes=16 * MB),
        cost_estimate=cost(2),
        name="select",
    )(where, *lists, y)


UNROLL = 4
HEAD = 128


def correlate_kernel(first, last, kc, offset, *refs):
    where_ref, seg_ref, ya, yb, yc, yd, xa, xb, xc, xd, lag_ref, qual_ref = refs[:12]
    if first:
        out_ref, ybuf, xbuf, xrow, cross, sems = refs[12:]
        acc_ref = None
    else:
        acc_hbm, out_ref, ybuf, xbuf, xrow, cross, sems, acc_ref, scale, stage, osem = refs[12:]
    parts = ((0, HEAD), (HEAD, kc - HEAD))
    copies = []
    for k, (lo, size) in enumerate(parts):
        span = pl.ds(lo * 8, size * 8)
        some = []
        for j, ref in enumerate((ya, yb, yc, yd)):
            rows = span if j >= 2 else pl.ds((offset + lo) * 8, size * 8)
            some.append(pltpu.make_async_copy(ref.at[rows], ybuf.at[seg_ref[j], span], sems.at[k * 8 + j]))
        for j, ref in enumerate((xa, xb, xc, xd)):
            some.append(pltpu.make_async_copy(ref.at[:, span], xbuf.at[j, :, span], sems.at[k * 8 + 4 + j]))
        copies.append(some)
        for copy in some:
            copy.start()
    if not first:
        prefetch = pltpu.make_async_copy(acc_hbm, acc_ref, sems.at[16])
        prefetch.start()

    rowid = lax.broadcasted_iota(jnp.int32, (16, 256), 0) % GRP
    lane = lax.broadcasted_iota(jnp.int32, (16, 256), 1) % GRP
    keep = rowid == lane
    zero = jnp.zeros((16, 256), jnp.bfloat16)
    stay = (lax.broadcasted_iota(jnp.int32, (8, 128), 0) < 4) == (lax.broadcasted_iota(jnp.int32, (8, 128), 1) < 64)

    def pair(n, slot):
        for far in range(4):
            for near in range(4):
                tile = xbuf[far, near * 16 : near * 16 + 16, pl.ds(pl.multiple_of(n * 128, 128), 128)].astype(jnp.float32)
                for half in range(2):
                    part = tile[half * 8 : half * 8 + 8]
                    moved = pltpu.roll(pltpu.roll(part, 4, 0), 64, 1)
                    row = (far * 4 + near) * 8
                    xrow[slot, row : row + 8, half * 128 : half * 128 + 128] = jnp.where(stay, part, moved)
        prods = []
        for a in range(2):
            tiles = []
            for p in range(0, 64, 2):
                row = (p // 4) * 8 + a * 4 + p % 4
                two = jnp.concatenate(
                    [xrow[slot, pl.ds(row, 8, stride=0), :], xrow[slot, pl.ds(row + 1, 8, stride=0), :]], axis=0
                ).astype(jnp.bfloat16)
                tiles.append(jnp.where(keep, two, zero))
            lhs = jnp.concatenate(tiles, axis=0)
            base = pl.multiple_of((2 * n + a) * ROWS, ROWS)
            reim, imre = [], []
            for s in range(SDEV):
                yr = ybuf[s, pl.ds(base, 32), :]
                yi = ybuf[s, pl.ds(base + 32, 32), :]
                reim += [yr, yi]
                imre += [-yi, yr]
            right = jnp.concatenate([jnp.concatenate(reim, axis=0), jnp.concatenate(imre, axis=0)], axis=1)
            prods.append(jnp.dot(lhs, right, preferred_element_type=jnp.float32))
        off = pl.multiple_of(n * 16, 16)
        for p in range(64):
            both = jnp.concatenate([prods[0][8 * p : 8 * p + 8], prods[1][8 * p : 8 * p + 8]], axis=0)
            both = both.astype(jnp.bfloat16)
            cross[p, pl.ds(off, 16), :] = both[:, :128]
            cross[p, pl.ds(pl.multiple_of(kc + off, 16), 16), :] = both[:, 128:]

    def pairs(m, _):
        for v in range(UNROLL):
            pair(m * UNROLL + v, v)
        return 0

    for (lo, size), some in zip(parts, copies):
        for copy in some:
            copy.wait()
        lax.fori_loop(lo // 16 // UNROLL, (lo + size) // 16 // UNROLL, pairs, 0)
    table = lag_ref[...]
    if last:
        flags = []
        for far in range(4):
            for near in range(4):
                flags.append(xbuf[far, near * 16 : near * 16 + 4, kc * 8 - 128 :])
        flags = jnp.concatenate([f.astype(jnp.float32) for f in flags], axis=0)[:, 64:80].astype(jnp.bfloat16)
        quality = qual_ref[...].astype(jnp.float32).astype(jnp.bfloat16)
        count = jnp.dot(flags, quality, preferred_element_type=jnp.float32)
        scale[...] = 1.0 / jnp.maximum(count, 1.0)
        prefetch.wait()

    def flush(n, slot):
        return pltpu.make_async_copy(stage.at[slot], out_ref.at[:, pl.ds(pl.multiple_of(n * 8, 8), 8), :], osem.at[slot])

    def lags(n, _):
        spots = [where_ref[n * 8 + j] for j in range(8)]
        parts = []
        for q in range(4):
            right = jnp.concatenate([cross[spots[2 * q]], cross[spots[2 * q + 1]]], axis=1)
            prod = jnp.dot(table, right, preferred_element_type=jnp.float32)
            parts += [prod[:, :128], prod[:, 128:]]
        if last:
            slot = n % 2
            parts = [(part + acc_ref[p]) * scale[pl.ds(p, 1), :] for part, p in zip(parts, spots)]

            @pl.when(n >= 2)
            def _():
                flush(n - 2, slot).wait()

            stage[slot] = pltpu.einshape("itj->tij", jnp.stack(parts, axis=0))[:NLAG]
            flush(n, slot).start()
        else:
            for part, p in zip(parts, spots):
                out_ref[p] = part
        return 0

    lax.fori_loop(0, 8, lags, 0)
    if last:
        flush(6, 0).wait()
        flush(7, 1).wait()


def correlate(first, last, kc, offset, where, seg, ys, xs, table, qual_t, acc=None):
    smem = pl.BlockSpec(memory_space=pltpu.SMEM)
    hbm = pl.BlockSpec(memory_space=pl.ANY)
    vmem = pl.BlockSpec(memory_space=pltpu.VMEM)
    args = (where, seg, *ys, *xs, table, qual_t)
    in_specs = [smem, smem] + [hbm] * 8 + [vmem, vmem]
    scratch = [
        pltpu.VMEM((4, kc * 8, 128), jnp.bfloat16),
        pltpu.VMEM((4, 64, kc * 8), jnp.bfloat16),
        pltpu.VMEM((UNROLL, 128, 256), jnp.float32),
        pltpu.VMEM((64, 2 * kc, 128), jnp.bfloat16),
        pltpu.SemaphoreType.DMA((17,)),
    ]
    if first:
        out_shape, out_specs = (64, TAU, 128), vmem
    else:
        out_shape, out_specs = (NLAG, 64, 128), hbm
        args += (acc,)
        in_specs += [hbm]
        scratch += [
            pltpu.VMEM((64, TAU, 128), jnp.float32),
            pltpu.VMEM((64, 128), jnp.float32),
            pltpu.VMEM((2, NLAG, 8, 128), jnp.float32),
            pltpu.SemaphoreType.DMA((2,)),
        ]
    return pl.pallas_call(
        functools.partial(correlate_kernel, first, last, kc, offset),
        out_shape=jax.ShapeDtypeStruct(out_shape, jnp.float32),
        in_specs=in_specs,
        out_specs=out_specs,
        scratch_shapes=scratch,
        compiler_params=pltpu.CompilerParams(vmem_limit_bytes=60 * MB),
        cost_estimate=cost(kc / 40),
        name="correlate_first" if first else "correlate_last",
    )(*args)


AXES = ("zhi", "core", "y", "zlo", "x")
SIZES = (2, 2, 4, 2, 4)


def permutation(move):
    out = []
    for flat in range(128):
        at = list(np.unravel_index(flat, SIZES))
        to = move(*[int(v) for v in at])
        out.append((flat, int(np.ravel_multi_index([v % n for v, n in zip(to, SIZES)], SIZES))))
    return out


def send(value, move):
    return lax.ppermute(value, AXES, permutation(move))


def sibling(zhi, core, y, zlo, x):
    return zhi, core + 1, y, zlo, x


def across(zhi, core, y, zlo, x):
    return zhi + 1, core, y, zlo, x


def ring(phase, d):
    def move(zhi, core, y, zlo, x):
        if core == phase:
            return zhi, core, y, zlo, x + d
        return zhi, core, y + d, zlo, x

    return move


def both(zhi, core, y, zlo, x):
    return zhi + 1, core + 1, y, zlo, x


def on_device(traces, src_index, quality):
    samples = jnp.transpose(traces, (1, 2, 0))
    qual_t = jnp.transpose(quality, (1, 0))
    zhi, core, yy, zlo, xx = [lax.axis_index(a) for a in AXES]
    me = zhi * 2 + core
    spot = jnp.stack([me, yy * 8 + zlo * 4 + xx])
    i = jnp.arange(64, dtype=jnp.int32)
    dx, dy = (xx - i % 4) % 4, (yy - (i // 8) % 4) % 4
    dx, dy = dx % 2 * 2 + dx // 2, dy % 2 * 2 + dy // 2
    far_step, near_step = jnp.where(core == 0, dy, dx), jnp.where(core == 0, dx, dy)
    where = far_step * 16 + near_step * 4 + (i // 4) % 2 * 2 + i // 32
    seg = jnp.bitwise_xor(me, jnp.arange(4, dtype=jnp.int32))
    table = lag_table(1000)
    tables, start = [], 0
    for kc in CHUNKS:
        tables.append(jnp.asarray(np.ascontiguousarray(table[:, :, start : start + kc]).reshape(TAU, 2 * kc)))
        start += kc

    lists = [src_index] + [send(src_index, move) for move in (sibling, across, both)]
    y0, y1, y = spectra(samples, qual_t, spot)

    slots = select(spot, lists, y).reshape(8, 2, -1)
    got = lax.all_to_all(slots, ("zhi", "core", "zlo"), 0, 0, tiled=False)
    y0, y1, y, got = lax.optimization_barrier((y0, y1, y, got))
    got = got.reshape(16, -1)
    far0 = send(y0, across)
    far1 = send(y1, across)
    pieces = [got] + [send(got, ring(0, d)) for d in (2, 1, 3)]
    *pieces, y = lax.optimization_barrier((*pieces, y))
    near = send(y, sibling)
    lines, start = [], 0
    for kc in CHUNKS:
        lines.append(jnp.concatenate([piece[:, start * 8 : (start + kc) * 8] for piece in pieces], axis=0))
        start += kc
    xs0 = [lines[0]] + [send(lines[0], ring(1, d)) for d in (2, 1, 3)]
    *xs0, line1, far0 = lax.optimization_barrier((*xs0, lines[1], far0))
    xs1 = [line1] + [send(line1, ring(1, d)) for d in (2, 1, 3)]
    acc = correlate(
        True, False, CHUNKS[0], 0, where, seg, (y, near, far0, send(far0, sibling)), xs0, tables[0], qual_t
    )
    far1, acc, *xs1 = lax.optimization_barrier((far1, acc, *xs1))
    out = correlate(
        False, True, CHUNKS[1], CHUNKS[0], where, seg, (y, near, far1, send(far1, sibling)), xs1, tables[1], qual_t, acc
    )
    return jnp.transpose(out, (1, 0, 2))


def solution(mesh):
    fine = Mesh(mesh.devices.reshape(2, 2, 4, 2, 4), ("zhi", "core", "y", "zlo", "x"))
    rcv = ("y", "zlo", "x")
    src = ("zhi", "core")
    return jax.shard_map(
        on_device,
        mesh=fine,
        in_specs=(P(rcv, src, None), P(src), P(rcv, None)),
        out_specs=P(src, None, rcv),
        check_vma=False,
    )
```

```python
import functools
import math

import jax
import jax.numpy as jnp
import ml_dtypes
import numpy as np
from jax import lax
from jax.experimental import pallas as pl
from jax.experimental.pallas import tpu as pltpu
from jax.sharding import Mesh, PartitionSpec as P

LAGH = 100
NLAG = 2 * LAGH + 1
TAU = 208
GRP = 8
KPAD = 1024
NGRP = KPAD // GRP
SDEV = 4
ROWS = 64
MB = 1 << 20


def start_tables(length):
    bins = np.arange(1, GRP + 1, dtype=np.float64)
    times = np.arange(length, dtype=np.float64)
    phase = 2.0 * math.pi / length * ((bins[:, None] * times[None, :]) % length)
    step = 2.0 * math.pi / length * ((GRP * times) % length)
    step = np.broadcast_to(step[None, :], phase.shape)
    return np.stack([np.cos(phase), -np.sin(phase), np.cos(step), np.sin(step)]).astype(np.float32)


def lag_table(half):
    bins = np.arange(1, half + 1, dtype=np.int64)
    lags = np.arange(-LAGH, LAGH + 1, dtype=np.int64)
    phase = 2.0 * math.pi / (2 * half) * ((lags[:, None] * bins[None, :]) % (2 * half))
    weight = np.where(bins == half, 1.0, 2.0)[None, :] / math.sqrt(half)
    out = np.zeros((TAU, 2, KPAD), np.float32)
    out[:NLAG, 0, :half] = weight * np.cos(phase)
    out[:NLAG, 1, :half] = -weight * np.sin(phase)
    return out.astype(ml_dtypes.bfloat16)


def cost(us):
    return pl.CostEstimate(flops=int(us * 1.1e9), transcendentals=0, bytes_accessed=1024)


DBLK = 25
CHUNKS = (640, 384)


def spectra_kernel(
    half, me_ref, ia, ib, ic, id_, x_hbm, start_hbm, qual_ref, y0_hbm, y1_hbm, y_hbm, sel_ref,
    x_ref, start_ref, y_ref, state, table, spec, power, sems,
):
    ngrp = half // GRP
    length = 2 * half
    blocks = ngrp // DBLK
    me, r = me_ref[0], me_ref[1]
    load_start = pltpu.make_async_copy(start_hbm, start_ref, sems.at[0])
    load_start.start()
    load = pltpu.make_async_copy(x_hbm, x_ref, sems.at[1])
    load.start()
    load_start.wait()

    def gen(slot):
        for lo in range(0, length, 128):
            cols = slice(lo, min(lo + 128, length))
            cos, sin = state[0, :, cols], state[1, :, cols]
            rc, rs = start_ref[2, :, cols], start_ref[3, :, cols]
            for n in range(DBLK):
                table[slot, n * 16 : n * 16 + 16, cols] = jnp.concatenate([cos, sin], axis=0).astype(jnp.bfloat16)
                cos, sin = cos * rc + sin * rs, sin * rc - cos * rs
            state[0, :, cols] = cos
            state[1, :, cols] = sin

    state[0] = start_ref[0]
    state[1] = start_ref[1]
    power[...] = jnp.zeros_like(power)
    gen(0)
    load.wait()
    samples = jnp.concatenate([x_ref[g] for g in range(4)], axis=1)

    def block(b, _):
        slot = b % 2
        prod = jnp.dot(table[slot], samples, preferred_element_type=jnp.float32)
        gen(1 - slot)
        spec[pl.ds(pl.multiple_of(b * (DBLK * 16), DBLK * 16), DBLK * 16), :] = prod
        power[...] += jnp.sum((prod * prod).reshape(DBLK * 2, 8, 512), axis=0)
        return 0

    lax.fori_loop(0, blocks, block, 0)
    mean = jnp.sum(power[...], axis=0, keepdims=True) * (1.0 / half)
    level2 = 0.25 * (mean + 1e-06)
    own = [qual_ref[pl.ds(me * 4 + g, 1), :].astype(jnp.float32) for g in range(4)]

    def whiten(n):
        base = pl.multiple_of(n * 16, 16)
        reals, imags = [], []
        for g in range(4):
            cols = slice(g * 128, (g + 1) * 128)
            real = spec[pl.ds(base, 8), cols]
            imag = spec[pl.ds(base + 8, 8), cols]
            inv = lax.rsqrt(jnp.maximum(real * real + imag * imag, level2[:, cols])) * own[g]
            reals.append(real * inv)
            imags.append(imag * inv)
        value = jnp.concatenate(reals + imags, axis=0).astype(jnp.bfloat16)
        y_ref[pl.ds(pl.multiple_of(n * ROWS, ROWS), ROWS), :] = value

    first = CHUNKS[0] // GRP

    def sweep(lo, hi):
        def some(m, _):
            for v in range(5):
                whiten(lo + m * 5 + v)
            return 0

        lax.fori_loop(0, (hi - lo) // 5, some, 0)

    row = lax.broadcasted_iota(jnp.int32, (8, 128), 0)
    lane = lax.broadcasted_iota(jnp.int32, (8, 128), 1)
    hot = jnp.zeros((8, 128), jnp.float32)
    for rel, ref in enumerate((ia, ib, ic, id_)):
        for h in range(2):
            here = (row == rel * 2 + h) & (lane == ref[r + 32 * h] - r * 128)
            hot = jnp.where(here, 1.0, hot)
    hot = hot.astype(jnp.bfloat16)

    def finish(lo, hi, part_hbm, k):
        span = pl.ds(lo * ROWS, (hi - lo) * ROWS)
        copies = [
            pltpu.make_async_copy(y_ref.at[span], part_hbm, sems.at[2 * k]),
            pltpu.make_async_copy(y_ref.at[span], y_hbm.at[span], sems.at[2 * k + 1]),
        ]
        for copy in copies:
            copy.start()
        value = y_ref[lo * ROWS : hi * ROWS, :]
        picked = lax.dot_general(hot, value, (((1,), (1,)), ((), ())), preferred_element_type=jnp.float32)
        picked = picked.astype(jnp.bfloat16)
        for rel in range(4):
            sel_ref[rel, :, lo * ROWS : hi * ROWS] = picked[rel * 2 : rel * 2 + 2]
        return copies

    first = CHUNKS[0] // GRP
    sweep(0, first)
    copies = finish(0, first, y0_hbm, 1)
    sweep(first, ngrp)
    y_ref[ngrp * ROWS :, :] = jnp.zeros(((NGRP - ngrp) * ROWS, 128), jnp.bfloat16)
    last = (NGRP - 1) * ROWS
    y_ref[last : last + 16, :] = qual_ref[...].astype(jnp.float32).astype(jnp.bfloat16)
    copies += finish(first, NGRP, y1_hbm, 2)
    for copy in copies:
        copy.wait()


def spectra(samples, qual_t, me, lists):
    length = samples.shape[1]
    half = length // 2
    start = jnp.asarray(start_tables(length))
    vmem = pl.BlockSpec(memory_space=pltpu.VMEM)
    smem = pl.BlockSpec(memory_space=pltpu.SMEM)
    hbm = pl.BlockSpec(memory_space=pltpu.HBM)
    return pl.pallas_call(
        functools.partial(spectra_kernel, half),
        out_shape=[
            jax.ShapeDtypeStruct((CHUNKS[0] * 8, 128), jnp.bfloat16),
            jax.ShapeDtypeStruct((CHUNKS[1] * 8, 128), jnp.bfloat16),
            jax.ShapeDtypeStruct((NGRP * ROWS, 128), jnp.bfloat16),
            jax.ShapeDtypeStruct((4, 2, NGRP * ROWS), jnp.bfloat16),
        ],
        in_specs=[smem] * 5 + [hbm, hbm, vmem],
        out_specs=[hbm, hbm, hbm, vmem],
        scratch_shapes=[
            pltpu.VMEM((4, length, 128), jnp.bfloat16),
            pltpu.VMEM((4, 8, length), jnp.float32),
            pltpu.VMEM((NGRP * ROWS, 128), jnp.bfloat16),
            pltpu.VMEM((2, 8, length), jnp.float32),
            pltpu.VMEM((2, DBLK * 16, length), jnp.bfloat16),
            pltpu.VMEM((2 * half, 512), jnp.float32),
            pltpu.VMEM((8, 512), jnp.float32),
            pltpu.SemaphoreType.DMA((6,)),
        ],
        compiler_params=pltpu.CompilerParams(vmem_limit_bytes=48 * MB),
        cost_estimate=cost(0.001),
        name="spectra",
    )(me, *lists, samples, start, qual_t)


def join_kernel(plan, count, *refs):
    for out, row, src, at in plan:
        value = refs[src][...].reshape(-1, refs[src].shape[-1]) if at is None else refs[src][at]
        refs[count + out][row : row + value.shape[0], :] = value


def join(values, plan, shapes, name):
    vmem = pl.BlockSpec(memory_space=pltpu.VMEM)
    return pl.pallas_call(
        functools.partial(join_kernel, plan, len(values)),
        out_shape=[jax.ShapeDtypeStruct(shape, values[0].dtype) for shape in shapes],
        in_specs=[vmem] * len(values),
        out_specs=[vmem] * len(shapes),
        compiler_params=pltpu.CompilerParams(vmem_limit_bytes=16 * MB),
        cost_estimate=cost(0.001),
        name=name,
    )(*values)


def split_kernel(pa, pb, pc, pd, line0, line1, sems):
    copies, start = [], 0
    for k, (line, kc) in enumerate(zip((line0, line1), CHUNKS)):
        for j, piece in enumerate((pa, pb, pc, pd)):
            copies.append(
                pltpu.make_async_copy(
                    piece.at[:, pl.ds(start * 8, kc * 8)], line.at[pl.ds(j * 16, 16), :], sems.at[k * 4 + j]
                )
            )
            copies[-1].start()
        start += kc
    for copy in copies:
        copy.wait()


def split(pieces):
    hbm = pl.BlockSpec(memory_space=pl.ANY)
    return pl.pallas_call(
        split_kernel,
        out_shape=[jax.ShapeDtypeStruct((64, kc * 8), jnp.bfloat16) for kc in CHUNKS],
        in_specs=[hbm] * 4,
        out_specs=[hbm] * 2,
        scratch_shapes=[pltpu.SemaphoreType.DMA((8,))],
        cost_estimate=cost(0.001),
        name="split",
    )(*pieces)


UNROLL = 4
HEAD = 128


def correlate_kernel(first, last, kc, offset, *refs):
    where_ref, ya, yb, yc, yd, xa, xb, xc, xd, lag_ref, qual_ref = refs[:11]
    if first:
        out_ref, ybuf, xbuf, xrow, cross, sems = refs[11:]
        acc_ref = None
    else:
        acc_hbm, out_ref, ybuf, xbuf, xrow, cross, sems, acc_ref, scale, stage, osem = refs[11:]
    parts = ((0, HEAD), (HEAD, kc - HEAD))
    copies = []
    for k, (lo, size) in enumerate(parts):
        span = pl.ds(lo * 8, size * 8)
        some = []
        for j, ref in enumerate((ya, yc, yb, yd)):
            rows = span if j % 2 else pl.ds((offset + lo) * 8, size * 8)
            some.append(pltpu.make_async_copy(ref.at[rows], ybuf.at[j, span], sems.at[k * 8 + j]))
        for j, ref in enumerate((xa, xb, xc, xd)):
            some.append(pltpu.make_async_copy(ref.at[:, span], xbuf.at[j, :, span], sems.at[k * 8 + 4 + j]))
        copies.append(some)
        for copy in some:
            copy.start()
    if not first:
        prefetch = pltpu.make_async_copy(acc_hbm, acc_ref, sems.at[16])
        prefetch.start()

    rowid = lax.broadcasted_iota(jnp.int32, (16, 256), 0) % GRP
    lane = lax.broadcasted_iota(jnp.int32, (16, 256), 1) % GRP
    keep = rowid == lane
    zero = jnp.zeros((16, 256), jnp.bfloat16)
    stay = (lax.broadcasted_iota(jnp.int32, (8, 128), 0) < 4) == (lax.broadcasted_iota(jnp.int32, (8, 128), 1) < 64)

    def pair(n, slot):
        for far in range(4):
            for near in range(4):
                tile = xbuf[far, near * 16 : near * 16 + 16, pl.ds(pl.multiple_of(n * 128, 128), 128)].astype(jnp.float32)
                for half in range(2):
                    part = tile[half * 8 : half * 8 + 8]
                    moved = pltpu.roll(pltpu.roll(part, 4, 0), 64, 1)
                    row = (far * 4 + near) * 8
                    xrow[slot, row : row + 8, half * 128 : half * 128 + 128] = jnp.where(stay, part, moved)
        prods = []
        for a in range(2):
            tiles = []
            for p in range(0, 64, 2):
                row = (p // 4) * 8 + a * 4 + p % 4
                two = jnp.concatenate(
                    [xrow[slot, pl.ds(row, 8, stride=0), :], xrow[slot, pl.ds(row + 1, 8, stride=0), :]], axis=0
                ).astype(jnp.bfloat16)
                tiles.append(jnp.where(keep, two, zero))
            lhs = jnp.concatenate(tiles, axis=0)
            base = pl.multiple_of((2 * n + a) * ROWS, ROWS)
            reim, imre = [], []
            for s in range(SDEV):
                yr = ybuf[s, pl.ds(base, 32), :]
                yi = ybuf[s, pl.ds(base + 32, 32), :]
                reim += [yr, yi]
                imre += [-yi, yr]
            right = jnp.concatenate([jnp.concatenate(reim, axis=0), jnp.concatenate(imre, axis=0)], axis=1)
            prods.append(jnp.dot(lhs, right, preferred_element_type=jnp.float32))
        off = pl.multiple_of(n * 16, 16)
        for p in range(64):
            both = jnp.concatenate([prods[0][8 * p : 8 * p + 8], prods[1][8 * p : 8 * p + 8]], axis=0)
            both = both.astype(jnp.bfloat16)
            cross[p, pl.ds(off, 16), :] = both[:, :128]
            cross[p, pl.ds(pl.multiple_of(kc + off, 16), 16), :] = both[:, 128:]

    def pairs(m, _):
        for v in range(UNROLL):
            pair(m * UNROLL + v, v)
        return 0

    for (lo, size), some in zip(parts, copies):
        for copy in some:
            copy.wait()
        lax.fori_loop(lo // 16 // UNROLL, (lo + size) // 16 // UNROLL, pairs, 0)
    table = lag_ref[...]
    if last:
        flags = []
        for far in range(4):
            for near in range(4):
                flags.append(xbuf[far, near * 16 : near * 16 + 4, kc * 8 - 128 :])
        flags = jnp.concatenate([f.astype(jnp.float32) for f in flags], axis=0)[:, 64:80].astype(jnp.bfloat16)
        quality = qual_ref[...].astype(jnp.float32).astype(jnp.bfloat16)
        count = jnp.dot(flags, quality, preferred_element_type=jnp.float32)
        scale[...] = 1.0 / jnp.maximum(count, 1.0)
        prefetch.wait()

    def flush(n, slot):
        return pltpu.make_async_copy(stage.at[slot], out_ref.at[:, pl.ds(pl.multiple_of(n * 8, 8), 8), :], osem.at[slot])

    def lags(n, _):
        spots = [where_ref[n * 8 + j] for j in range(8)]
        parts = []
        for q in range(4):
            right = jnp.concatenate([cross[spots[2 * q]], cross[spots[2 * q + 1]]], axis=1)
            prod = jnp.dot(table, right, preferred_element_type=jnp.float32)
            parts += [prod[:, :128], prod[:, 128:]]
        if last:
            slot = n % 2
            parts = [(part + acc_ref[p]) * scale[pl.ds(p, 1), :] for part, p in zip(parts, spots)]

            @pl.when(n >= 2)
            def _():
                flush(n - 2, slot).wait()

            stage[slot] = pltpu.einshape("itj->tij", jnp.stack(parts, axis=0))[:NLAG]
            flush(n, slot).start()
        else:
            for part, p in zip(parts, spots):
                out_ref[p] = part
        return 0

    lax.fori_loop(0, 8, lags, 0)
    if last:
        flush(6, 0).wait()
        flush(7, 1).wait()


def correlate(first, last, kc, offset, where, ys, xs, table, qual_t, acc=None):
    smem = pl.BlockSpec(memory_space=pltpu.SMEM)
    hbm = pl.BlockSpec(memory_space=pl.ANY)
    vmem = pl.BlockSpec(memory_space=pltpu.VMEM)
    args = (where, *ys, *xs, table, qual_t)
    in_specs = [smem] + [hbm] * 8 + [vmem, vmem]
    scratch = [
        pltpu.VMEM((4, kc * 8, 128), jnp.bfloat16),
        pltpu.VMEM((4, 64, kc * 8), jnp.bfloat16),
        pltpu.VMEM((UNROLL, 128, 256), jnp.float32),
        pltpu.VMEM((64, 2 * kc, 128), jnp.bfloat16),
        pltpu.SemaphoreType.DMA((17,)),
    ]
    if first:
        out_shape, out_specs = (64, TAU, 128), vmem
    else:
        out_shape, out_specs = (NLAG, 64, 128), hbm
        args += (acc,)
        in_specs += [hbm]
        scratch += [
            pltpu.VMEM((64, TAU, 128), jnp.float32),
            pltpu.VMEM((64, 128), jnp.float32),
            pltpu.VMEM((2, NLAG, 8, 128), jnp.float32),
            pltpu.SemaphoreType.DMA((2,)),
        ]
    return pl.pallas_call(
        functools.partial(correlate_kernel, first, last, kc, offset),
        out_shape=jax.ShapeDtypeStruct(out_shape, jnp.float32),
        in_specs=in_specs,
        out_specs=out_specs,
        scratch_shapes=scratch,
        compiler_params=pltpu.CompilerParams(vmem_limit_bytes=60 * MB),
        cost_estimate=cost(0.001),
        name="correlate_first" if first else "correlate_last",
    )(*args)


AXES = ("zhi", "core", "y", "zlo", "x")
SIZES = (2, 2, 4, 2, 4)


def permutation(move):
    out = []
    for flat in range(128):
        at = list(np.unravel_index(flat, SIZES))
        to = move(*[int(v) for v in at])
        out.append((flat, int(np.ravel_multi_index([v % n for v, n in zip(to, SIZES)], SIZES))))
    return out


def send(value, move):
    return lax.ppermute(value, AXES, permutation(move))


def sibling(zhi, core, y, zlo, x):
    return zhi, core + 1, y, zlo, x


def across(zhi, core, y, zlo, x):
    return zhi + 1, core, y, zlo, x


def ring(phase, d):
    def move(zhi, core, y, zlo, x):
        if core == phase:
            return zhi, core, y, zlo, x + d
        return zhi, core, y + d, zlo, x

    return move


def both(zhi, core, y, zlo, x):
    return zhi + 1, core + 1, y, zlo, x


def beside(zhi, core, y, zlo, x):
    return zhi, core, y, zlo + 1, x


def aside(zhi, core, y, zlo, x):
    return zhi + 1, core, y, zlo + 1, x


def on_device(traces, src_index, quality):
    samples = jnp.transpose(traces, (1, 2, 0))
    qual_t = jnp.transpose(quality, (1, 0))
    zhi, core, yy, zlo, xx = [lax.axis_index(a) for a in AXES]
    me = zhi * 2 + core
    spot = jnp.stack([me, yy * 8 + zlo * 4 + xx])
    i = jnp.arange(64, dtype=jnp.int32)
    dx, dy = (xx - i % 4) % 4, (yy - (i // 8) % 4) % 4
    dx, dy = dx % 2 * 2 + dx // 2, dy % 2 * 2 + dy // 2
    far_step, near_step = jnp.where(core == 0, dy, dx), jnp.where(core == 0, dx, dy)
    where = far_step * 16 + near_step * 4 + jnp.bitwise_xor((i // 4) % 2, zlo) * 2 + i // 32
    table = lag_table(1000)
    tables, start = [], 0
    for kc in CHUNKS:
        tables.append(jnp.asarray(np.ascontiguousarray(table[:, :, start : start + kc]).reshape(TAU, 2 * kc)))
        start += kc

    lists = [src_index] + [send(src_index, move) for move in (sibling, across, both)]
    y0, y1, y, sel = spectra(samples, qual_t, spot, lists)

    stay, away = sel[:2], sel[2:]
    out = [send(stay, beside), send(away, across), send(away, aside)]
    y0, y1, y, stay, *out = lax.optimization_barrier((y0, y1, y, stay, *out))
    far0 = send(y0, across)
    held = [stay] + out
    near = send(y, sibling)
    lanes = y.shape[0]
    both_cores = [(part, j * 2, j, part) for part in range(2) for j in range(4)]
    mine, theirs = join(held, both_cores, [(8, lanes)] * 2, "join_column")
    theirs = send(theirs, sibling)
    (got,) = join((mine, theirs), [(0, 0, 0, None), (0, 8, 1, None)], [(16, lanes)], "join_cores")
    pieces = [got] + [send(got, ring(0, d)) for d in (2, 1, 3)]
    *pieces, near, y1 = lax.optimization_barrier((*pieces, near, y1))
    far1 = send(y1, across)
    lines = split(pieces)
    xs0 = [lines[0]] + [send(lines[0], ring(1, d)) for d in (2, 1, 3)]
    *xs0, line1 = lax.optimization_barrier((*xs0, lines[1]))
    far0 = lax.optimization_barrier((far0, lines[1]))[0]
    xs1 = [line1] + [send(line1, ring(1, d)) for d in (2, 1, 3)]
    acc = correlate(
        True, False, CHUNKS[0], 0, where, (y, near, far0, send(far0, sibling)), xs0, tables[0], qual_t
    )
    far1, acc, *xs1 = lax.optimization_barrier((far1, acc, *xs1))
    out = correlate(
        False, True, CHUNKS[1], CHUNKS[0], where, (y, near, far1, send(far1, sibling)), xs1, tables[1], qual_t, acc
    )
    return jnp.transpose(out, (1, 0, 2))


def solution(mesh):
    fine = Mesh(mesh.devices.reshape(2, 2, 4, 2, 4), ("zhi", "core", "y", "zlo", "x"))
    rcv = ("y", "zlo", "x")
    src = ("zhi", "core")
    return jax.shard_map(
        on_device,
        mesh=fine,
        in_specs=(P(rcv, src, None), P(src), P(rcv, None)),
        out_specs=P(src, None, rcv),
        check_vma=False,
    )
```

```python
import functools
import math

import jax
import jax.numpy as jnp
import ml_dtypes
import numpy as np
from jax import lax
from jax.experimental import pallas as pl
from jax.experimental.pallas import tpu as pltpu
from jax.sharding import Mesh, PartitionSpec as P

LAGH = 100
NLAG = 2 * LAGH + 1
TAU = 208
GRP = 8
KPAD = 1024
NGRP = KPAD // GRP
SDEV = 4
ROWS = 64
MB = 1 << 20


def start_tables(length):
    bins = np.arange(1, GRP + 1, dtype=np.float64)
    times = np.arange(length, dtype=np.float64)
    phase = 2.0 * math.pi / length * ((bins[:, None] * times[None, :]) % length)
    step = 2.0 * math.pi / length * ((GRP * times) % length)
    step = np.broadcast_to(step[None, :], phase.shape)
    return np.stack([np.cos(phase), -np.sin(phase), np.cos(step), np.sin(step)]).astype(np.float32)


def lag_table(half):
    bins = np.arange(1, half + 1, dtype=np.int64)
    lags = np.arange(-LAGH, LAGH + 1, dtype=np.int64)
    phase = 2.0 * math.pi / (2 * half) * ((lags[:, None] * bins[None, :]) % (2 * half))
    weight = np.where(bins == half, 1.0, 2.0)[None, :] / math.sqrt(half)
    out = np.zeros((TAU, 2, KPAD), np.float32)
    out[:NLAG, 0, :half] = weight * np.cos(phase)
    out[:NLAG, 1, :half] = -weight * np.sin(phase)
    return out.astype(ml_dtypes.bfloat16)


def cost(us):
    return pl.CostEstimate(flops=int(us * 1.1e9), transcendentals=0, bytes_accessed=1024)


DBLK = 25
CHUNKS = (384, 640)


def spectra_kernel(
    half, me_ref, ia, ib, ic, id_, x_hbm, start_hbm, qual_ref, y0_hbm, y1_hbm, y_hbm, sel_ref,
    x_ref, start_ref, y_ref, state, table, spec, power, sems,
):
    ngrp = half // GRP
    length = 2 * half
    blocks = ngrp // DBLK
    me, r = me_ref[0], me_ref[1]
    load_start = pltpu.make_async_copy(start_hbm, start_ref, sems.at[0])
    load_start.start()
    load = pltpu.make_async_copy(x_hbm, x_ref, sems.at[1])
    load.start()
    load_start.wait()

    def gen(slot):
        for lo in range(0, length, 128):
            cols = slice(lo, min(lo + 128, length))
            cos, sin = state[0, :, cols], state[1, :, cols]
            rc, rs = start_ref[2, :, cols], start_ref[3, :, cols]
            for n in range(DBLK):
                table[slot, n * 16 : n * 16 + 16, cols] = jnp.concatenate([cos, sin], axis=0).astype(jnp.bfloat16)
                cos, sin = cos * rc + sin * rs, sin * rc - cos * rs
            state[0, :, cols] = cos
            state[1, :, cols] = sin

    state[0] = start_ref[0]
    state[1] = start_ref[1]
    power[...] = jnp.zeros_like(power)
    gen(0)
    load.wait()
    samples = jnp.concatenate([x_ref[g] for g in range(4)], axis=1)

    def block(b, _):
        slot = b % 2
        prod = jnp.dot(table[slot], samples, preferred_element_type=jnp.float32)
        gen(1 - slot)
        spec[pl.ds(pl.multiple_of(b * (DBLK * 16), DBLK * 16), DBLK * 16), :] = prod
        power[...] += jnp.sum((prod * prod).reshape(DBLK * 2, 8, 512), axis=0)
        return 0

    lax.fori_loop(0, blocks, block, 0)
    mean = jnp.sum(power[...], axis=0, keepdims=True) * (1.0 / half)
    level2 = 0.25 * (mean + 1e-06)
    own = [qual_ref[pl.ds(me * 4 + g, 1), :].astype(jnp.float32) for g in range(4)]

    def whiten(n):
        base = pl.multiple_of(n * 16, 16)
        reals, imags = [], []
        for g in range(4):
            cols = slice(g * 128, (g + 1) * 128)
            real = spec[pl.ds(base, 8), cols]
            imag = spec[pl.ds(base + 8, 8), cols]
            inv = lax.rsqrt(jnp.maximum(real * real + imag * imag, level2[:, cols])) * own[g]
            reals.append(real * inv)
            imags.append(imag * inv)
        value = jnp.concatenate(reals + imags, axis=0).astype(jnp.bfloat16)
        y_ref[pl.ds(pl.multiple_of(n * ROWS, ROWS), ROWS), :] = value

    first = CHUNKS[0] // GRP

    def sweep(lo, hi):
        def some(m, _):
            for v in range(5):
                whiten(lo + m * 5 + v)
            return 0

        lax.fori_loop(0, (hi - lo) // 5, some, 0)
        for n in range(hi - (hi - lo) % 5, hi):
            whiten(n)

    row = lax.broadcasted_iota(jnp.int32, (8, 128), 0)
    lane = lax.broadcasted_iota(jnp.int32, (8, 128), 1)
    hot = jnp.zeros((8, 128), jnp.float32)
    for rel, ref in enumerate((ia, ib, ic, id_)):
        for h in range(2):
            here = (row == rel * 2 + h) & (lane == ref[r + 32 * h] - r * 128)
            hot = jnp.where(here, 1.0, hot)
    hot = hot.astype(jnp.bfloat16)

    def finish(lo, hi, part_hbm, k):
        span = pl.ds(lo * ROWS, (hi - lo) * ROWS)
        copies = [
            pltpu.make_async_copy(y_ref.at[span], part_hbm, sems.at[2 * k]),
            pltpu.make_async_copy(y_ref.at[span], y_hbm.at[span], sems.at[2 * k + 1]),
        ]
        for copy in copies:
            copy.start()
        value = y_ref[lo * ROWS : hi * ROWS, :]
        picked = lax.dot_general(hot, value, (((1,), (1,)), ((), ())), preferred_element_type=jnp.float32)
        picked = picked.astype(jnp.bfloat16)
        for rel in range(4):
            sel_ref[rel, :, lo * ROWS : hi * ROWS] = picked[rel * 2 : rel * 2 + 2]
        return copies

    first = CHUNKS[0] // GRP
    sweep(0, first)
    copies = finish(0, first, y0_hbm, 1)
    sweep(first, ngrp)
    y_ref[ngrp * ROWS :, :] = jnp.zeros(((NGRP - ngrp) * ROWS, 128), jnp.bfloat16)
    last = (NGRP - 1) * ROWS
    y_ref[last : last + 16, :] = qual_ref[...].astype(jnp.float32).astype(jnp.bfloat16)
    copies += finish(first, NGRP, y1_hbm, 2)
    for copy in copies:
        copy.wait()


def spectra(samples, qual_t, me, lists):
    length = samples.shape[1]
    half = length // 2
    start = jnp.asarray(start_tables(length))
    vmem = pl.BlockSpec(memory_space=pltpu.VMEM)
    smem = pl.BlockSpec(memory_space=pltpu.SMEM)
    hbm = pl.BlockSpec(memory_space=pltpu.HBM)
    return pl.pallas_call(
        functools.partial(spectra_kernel, half),
        out_shape=[
            jax.ShapeDtypeStruct((CHUNKS[0] * 8, 128), jnp.bfloat16),
            jax.ShapeDtypeStruct((CHUNKS[1] * 8, 128), jnp.bfloat16),
            jax.ShapeDtypeStruct((NGRP * ROWS, 128), jnp.bfloat16),
            jax.ShapeDtypeStruct((4, 2, NGRP * ROWS), jnp.bfloat16),
        ],
        in_specs=[smem] * 5 + [hbm, hbm, vmem],
        out_specs=[hbm, hbm, hbm, vmem],
        scratch_shapes=[
            pltpu.VMEM((4, length, 128), jnp.bfloat16),
            pltpu.VMEM((4, 8, length), jnp.float32),
            pltpu.VMEM((NGRP * ROWS, 128), jnp.bfloat16),
            pltpu.VMEM((2, 8, length), jnp.float32),
            pltpu.VMEM((2, DBLK * 16, length), jnp.bfloat16),
            pltpu.VMEM((2 * half, 512), jnp.float32),
            pltpu.VMEM((8, 512), jnp.float32),
            pltpu.SemaphoreType.DMA((6,)),
        ],
        compiler_params=pltpu.CompilerParams(vmem_limit_bytes=63 * MB),
        cost_estimate=cost(0.001),
        name="spectra",
    )(me, *lists, samples, start, qual_t)


def join_kernel(plan, count, *refs):
    for out, row, src, at in plan:
        value = refs[src][...].reshape(-1, refs[src].shape[-1]) if at is None else refs[src][at]
        refs[count + out][row : row + value.shape[0], :] = value


def join(values, plan, shapes, name):
    vmem = pl.BlockSpec(memory_space=pltpu.VMEM)
    return pl.pallas_call(
        functools.partial(join_kernel, plan, len(values)),
        out_shape=[jax.ShapeDtypeStruct(shape, values[0].dtype) for shape in shapes],
        in_specs=[vmem] * len(values),
        out_specs=[vmem] * len(shapes),
        compiler_params=pltpu.CompilerParams(vmem_limit_bytes=16 * MB),
        cost_estimate=cost(0.001),
        name=name,
    )(*values)


def lines_kernel(pa, pb, pc, pd, *lines):
    start = 0
    for line, kc in zip(lines, CHUNKS):
        for j, piece in enumerate((pa, pb, pc, pd)):
            line[j * 16 : j * 16 + 16, :] = piece[:, start * 8 : (start + kc) * 8]
        start += kc


def split(pieces):
    vmem = pl.BlockSpec(memory_space=pltpu.VMEM)
    return pl.pallas_call(
        lines_kernel,
        out_shape=[jax.ShapeDtypeStruct((64, kc * 8), jnp.bfloat16) for kc in CHUNKS],
        in_specs=[vmem] * 4,
        out_specs=[vmem] * 2,
        compiler_params=pltpu.CompilerParams(vmem_limit_bytes=16 * MB),
        cost_estimate=cost(0.001),
        name="split",
    )(*pieces)


UNROLL = 4
HEAD = 128


def correlate_kernel(first, last, kc, offset, *refs):
    where_ref, ya, yb, yc, yd, xa, xb, xc, xd, lag_ref, qual_ref = refs[:11]
    if first:
        out_ref, ybuf, xbuf, xrow, cross, sems = refs[11:]
        acc_ref = None
    else:
        acc_hbm, out_ref, ybuf, xbuf, xrow, cross, sems, acc_ref, scale, stage, osem = refs[11:]
    parts = ((0, HEAD), (HEAD, kc - HEAD))
    copies = []
    for k, (lo, size) in enumerate(parts):
        span = pl.ds(lo * 8, size * 8)
        some = []
        for j, ref in enumerate((ya, yc, yb, yd)):
            rows = span if j % 2 else pl.ds((offset + lo) * 8, size * 8)
            some.append(pltpu.make_async_copy(ref.at[rows], ybuf.at[j, span], sems.at[k * 8 + j]))
        for j, ref in enumerate((xa, xb, xc, xd)):
            some.append(pltpu.make_async_copy(ref.at[:, span], xbuf.at[j, :, span], sems.at[k * 8 + 4 + j]))
        copies.append(some)
        for copy in some:
            copy.start()
    if not first:
        prefetch = pltpu.make_async_copy(acc_hbm, acc_ref, sems.at[16])
        prefetch.start()

    rowid = lax.broadcasted_iota(jnp.int32, (16, 256), 0) % GRP
    lane = lax.broadcasted_iota(jnp.int32, (16, 256), 1) % GRP
    keep = rowid == lane
    zero = jnp.zeros((16, 256), jnp.bfloat16)
    stay = (lax.broadcasted_iota(jnp.int32, (8, 128), 0) < 4) == (lax.broadcasted_iota(jnp.int32, (8, 128), 1) < 64)

    def pair(n, slot):
        for far in range(4):
            for near in range(4):
                tile = xbuf[far, near * 16 : near * 16 + 16, pl.ds(pl.multiple_of(n * 128, 128), 128)].astype(jnp.float32)
                for half in range(2):
                    part = tile[half * 8 : half * 8 + 8]
                    moved = pltpu.roll(pltpu.roll(part, 4, 0), 64, 1)
                    row = (far * 4 + near) * 8
                    xrow[slot, row : row + 8, half * 128 : half * 128 + 128] = jnp.where(stay, part, moved)
        prods = []
        for a in range(2):
            tiles = []
            for p in range(0, 64, 2):
                row = (p // 4) * 8 + a * 4 + p % 4
                two = jnp.concatenate(
                    [xrow[slot, pl.ds(row, 8, stride=0), :], xrow[slot, pl.ds(row + 1, 8, stride=0), :]], axis=0
                ).astype(jnp.bfloat16)
                tiles.append(jnp.where(keep, two, zero))
            lhs = jnp.concatenate(tiles, axis=0)
            base = pl.multiple_of((2 * n + a) * ROWS, ROWS)
            reim, imre = [], []
            for s in range(SDEV):
                yr = ybuf[s, pl.ds(base, 32), :]
                yi = ybuf[s, pl.ds(base + 32, 32), :]
                reim += [yr, yi]
                imre += [-yi, yr]
            right = jnp.concatenate([jnp.concatenate(reim, axis=0), jnp.concatenate(imre, axis=0)], axis=1)
            prods.append(jnp.dot(lhs, right, preferred_element_type=jnp.float32))
        off = pl.multiple_of(n * 16, 16)
        for p in range(64):
            both = jnp.concatenate([prods[0][8 * p : 8 * p + 8], prods[1][8 * p : 8 * p + 8]], axis=0)
            both = both.astype(jnp.bfloat16)
            cross[p, pl.ds(off, 16), :] = both[:, :128]
            cross[p, pl.ds(pl.multiple_of(kc + off, 16), 16), :] = both[:, 128:]

    def pairs(m, _):
        for v in range(UNROLL):
            pair(m * UNROLL + v, v)
        return 0

    for (lo, size), some in zip(parts, copies):
        for copy in some:
            copy.wait()
        lax.fori_loop(lo // 16 // UNROLL, (lo + size) // 16 // UNROLL, pairs, 0)
    table = lag_ref[...]
    if last:
        flags = []
        for far in range(4):
            for near in range(4):
                flags.append(xbuf[far, near * 16 : near * 16 + 4, kc * 8 - 128 :])
        flags = jnp.concatenate([f.astype(jnp.float32) for f in flags], axis=0)[:, 64:80].astype(jnp.bfloat16)
        quality = qual_ref[...].astype(jnp.float32).astype(jnp.bfloat16)
        count = jnp.dot(flags, quality, preferred_element_type=jnp.float32)
        scale[...] = 1.0 / jnp.maximum(count, 1.0)
        prefetch.wait()

    def flush(n, slot):
        return pltpu.make_async_copy(stage.at[slot], out_ref.at[:, pl.ds(pl.multiple_of(n * 8, 8), 8), :], osem.at[slot])

    def lags(n, _):
        spots = [where_ref[n * 8 + j] for j in range(8)]
        parts = []
        for q in range(4):
            right = jnp.concatenate([cross[spots[2 * q]], cross[spots[2 * q + 1]]], axis=1)
            prod = jnp.dot(table, right, preferred_element_type=jnp.float32)
            parts += [prod[:, :128], prod[:, 128:]]
        if last:
            slot = n % 2
            parts = [(part + acc_ref[p]) * scale[pl.ds(p, 1), :] for part, p in zip(parts, spots)]

            @pl.when(n >= 2)
            def _():
                flush(n - 2, slot).wait()

            stage[slot] = pltpu.einshape("itj->tij", jnp.stack(parts, axis=0))[:NLAG]
            flush(n, slot).start()
        else:
            for part, p in zip(parts, spots):
                out_ref[p] = part
        return 0

    lax.fori_loop(0, 8, lags, 0)
    if last:
        flush(6, 0).wait()
        flush(7, 1).wait()


def correlate(first, last, kc, offset, where, ys, xs, table, qual_t, acc=None):
    smem = pl.BlockSpec(memory_space=pltpu.SMEM)
    hbm = pl.BlockSpec(memory_space=pl.ANY)
    vmem = pl.BlockSpec(memory_space=pltpu.VMEM)
    args = (where, *ys, *xs, table, qual_t)
    in_specs = [smem] + [hbm] * 8 + [vmem, vmem]
    scratch = [
        pltpu.VMEM((4, kc * 8, 128), jnp.bfloat16),
        pltpu.VMEM((4, 64, kc * 8), jnp.bfloat16),
        pltpu.VMEM((UNROLL, 128, 256), jnp.float32),
        pltpu.VMEM((64, 2 * kc, 128), jnp.bfloat16),
        pltpu.SemaphoreType.DMA((17,)),
    ]
    if first:
        out_shape, out_specs = (64, TAU, 128), vmem
    else:
        out_shape, out_specs = (NLAG, 64, 128), hbm
        args += (acc,)
        in_specs += [hbm]
        scratch += [
            pltpu.VMEM((64, TAU, 128), jnp.float32),
            pltpu.VMEM((64, 128), jnp.float32),
            pltpu.VMEM((2, NLAG, 8, 128), jnp.float32),
            pltpu.SemaphoreType.DMA((2,)),
        ]
    return pl.pallas_call(
        functools.partial(correlate_kernel, first, last, kc, offset),
        out_shape=jax.ShapeDtypeStruct(out_shape, jnp.float32),
        in_specs=in_specs,
        out_specs=out_specs,
        scratch_shapes=scratch,
        compiler_params=pltpu.CompilerParams(vmem_limit_bytes=60 * MB),
        cost_estimate=cost(0.001),
        name="correlate_first" if first else "correlate_last",
    )(*args)


AXES = ("zhi", "core", "y", "zlo", "x")
SIZES = (2, 2, 4, 2, 4)


def permutation(move):
    out = []
    for flat in range(128):
        at = list(np.unravel_index(flat, SIZES))
        to = move(*[int(v) for v in at])
        out.append((flat, int(np.ravel_multi_index([v % n for v, n in zip(to, SIZES)], SIZES))))
    return out


def send(value, move):
    return lax.ppermute(value, AXES, permutation(move))


def sibling(zhi, core, y, zlo, x):
    return zhi, core + 1, y, zlo, x


def across(zhi, core, y, zlo, x):
    return zhi + 1, core, y, zlo, x


def ring(phase, d):
    def move(zhi, core, y, zlo, x):
        if core == phase:
            return zhi, core, y, zlo, x + d
        return zhi, core, y + d, zlo, x

    return move


def both(zhi, core, y, zlo, x):
    return zhi + 1, core + 1, y, zlo, x


def beside(zhi, core, y, zlo, x):
    return zhi, core, y, zlo + 1, x


def aside(zhi, core, y, zlo, x):
    return zhi + 1, core, y, zlo + 1, x


def on_device(traces, src_index, quality):
    samples = jnp.transpose(traces, (1, 2, 0))
    qual_t = jnp.transpose(quality, (1, 0))
    zhi, core, yy, zlo, xx = [lax.axis_index(a) for a in AXES]
    me = zhi * 2 + core
    spot = jnp.stack([me, yy * 8 + zlo * 4 + xx])
    i = jnp.arange(64, dtype=jnp.int32)
    dx, dy = (xx - i % 4) % 4, (yy - (i // 8) % 4) % 4
    dx, dy = dx % 2 * 2 + dx // 2, dy % 2 * 2 + dy // 2
    far_step, near_step = jnp.where(core == 0, dy, dx), jnp.where(core == 0, dx, dy)
    where = far_step * 16 + near_step * 4 + jnp.bitwise_xor((i // 4) % 2, zlo) * 2 + i // 32
    table = lag_table(1000)
    tables, start = [], 0
    for kc in CHUNKS:
        tables.append(jnp.asarray(np.ascontiguousarray(table[:, :, start : start + kc]).reshape(TAU, 2 * kc)))
        start += kc

    lists = [src_index] + [send(src_index, move) for move in (sibling, across, both)]
    y0, y1, y, sel = spectra(samples, qual_t, spot, lists)

    stay, away = sel[:2], sel[2:]
    out = [send(stay, beside), send(away, across), send(away, aside)]
    y0, y1, y, stay, *out = lax.optimization_barrier((y0, y1, y, stay, *out))
    far0 = send(y0, across)
    held = [stay] + out
    near = send(y, sibling)
    lanes = y.shape[0]
    both_cores = [(part, j * 2, j, part) for part in range(2) for j in range(4)]
    mine, theirs = join(held, both_cores, [(8, lanes)] * 2, "join_column")
    theirs = send(theirs, sibling)
    (got,) = join((mine, theirs), [(0, 0, 0, None), (0, 8, 1, None)], [(16, lanes)], "join_cores")
    pieces = [got] + [send(got, ring(0, d)) for d in (2, 1, 3)]
    *pieces, near = lax.optimization_barrier((*pieces, near))
    far1 = send(y1, across)
    lines = split(pieces)
    xs0 = [lines[0]] + [send(lines[0], ring(1, d)) for d in (2, 1, 3)]
    *xs0, line1 = lax.optimization_barrier((*xs0, lines[1]))
    xs1 = [line1] + [send(line1, ring(1, d)) for d in (2, 1, 3)]
    acc = correlate(
        True, False, CHUNKS[0], 0, where, (y, near, far0, send(far0, sibling)), xs0, tables[0], qual_t
    )
    far1, acc, *xs1 = lax.optimization_barrier((far1, acc, *xs1))
    out = correlate(
        False, True, CHUNKS[1], CHUNKS[0], where, (y, near, far1, send(far1, sibling)), xs1, tables[1], qual_t, acc
    )
    return jnp.transpose(out, (1, 0, 2))


def solution(mesh):
    fine = Mesh(mesh.devices.reshape(2, 2, 4, 2, 4), ("zhi", "core", "y", "zlo", "x"))
    rcv = ("y", "zlo", "x")
    src = ("zhi", "core")
    return jax.shard_map(
        on_device,
        mesh=fine,
        in_specs=(P(rcv, src, None), P(src), P(rcv, None)),
        out_specs=P(src, None, rcv),
        check_vma=False,
    )
```

```python
import functools
import math

import jax
import jax.numpy as jnp
import ml_dtypes
import numpy as np
from jax import lax
from jax.experimental import pallas as pl
from jax.experimental.pallas import tpu as pltpu
from jax.sharding import Mesh, PartitionSpec as P

LAGH = 100
NLAG = 2 * LAGH + 1
TAU = 208
GRP = 8
KPAD = 1024
NGRP = KPAD // GRP
SDEV = 4
ROWS = 64
MB = 1 << 20


def start_tables(length):
    bins = np.arange(1, GRP + 1, dtype=np.float64)
    times = np.arange(length, dtype=np.float64)
    phase = 2.0 * math.pi / length * ((bins[:, None] * times[None, :]) % length)
    step = 2.0 * math.pi / length * ((GRP * times) % length)
    step = np.broadcast_to(step[None, :], phase.shape)
    return np.stack([np.cos(phase), -np.sin(phase), np.cos(step), np.sin(step)]).astype(np.float32)


def lag_table(half):
    bins = np.arange(1, half + 1, dtype=np.int64)
    lags = np.arange(-LAGH, LAGH + 1, dtype=np.int64)
    phase = 2.0 * math.pi / (2 * half) * ((lags[:, None] * bins[None, :]) % (2 * half))
    weight = np.where(bins == half, 1.0, 2.0)[None, :] / math.sqrt(half)
    out = np.zeros((TAU, 2, KPAD), np.float32)
    out[:NLAG, 0, :half] = weight * np.cos(phase)
    out[:NLAG, 1, :half] = -weight * np.sin(phase)
    return out.astype(ml_dtypes.bfloat16)


def cost(us):
    return pl.CostEstimate(flops=int(us * 1.1e9), transcendentals=0, bytes_accessed=1024)


DBLK = 25
CHUNKS = (384, 640)


def spectra_kernel(
    half, me_ref, ia, ib, ic, id_, x_hbm, start_hbm, qual_ref, y0_hbm, y1_hbm, y_hbm, stay_ref, away_ref,
    x_ref, start_ref, y_ref, state, table, spec, power, sems,
):
    ngrp = half // GRP
    length = 2 * half
    blocks = ngrp // DBLK
    me, r = me_ref[0], me_ref[1]
    load_start = pltpu.make_async_copy(start_hbm, start_ref, sems.at[0])
    load_start.start()
    load = pltpu.make_async_copy(x_hbm, x_ref, sems.at[1])
    load.start()
    load_start.wait()

    def gen(slot):
        for lo in range(0, length, 128):
            cols = slice(lo, min(lo + 128, length))
            cos, sin = state[0, :, cols], state[1, :, cols]
            rc, rs = start_ref[2, :, cols], start_ref[3, :, cols]
            for n in range(DBLK):
                table[slot, n * 16 : n * 16 + 16, cols] = jnp.concatenate([cos, sin], axis=0).astype(jnp.bfloat16)
                cos, sin = cos * rc + sin * rs, sin * rc - cos * rs
            state[0, :, cols] = cos
            state[1, :, cols] = sin

    state[0] = start_ref[0]
    state[1] = start_ref[1]
    power[...] = jnp.zeros_like(power)
    gen(0)
    load.wait()
    samples = jnp.concatenate([x_ref[g] for g in range(4)], axis=1)

    def block(b, _):
        slot = b % 2
        prod = jnp.dot(table[slot], samples, preferred_element_type=jnp.float32)
        gen(1 - slot)
        spec[pl.ds(pl.multiple_of(b * (DBLK * 16), DBLK * 16), DBLK * 16), :] = prod
        power[...] += jnp.sum((prod * prod).reshape(DBLK * 2, 8, 512), axis=0)
        return 0

    lax.fori_loop(0, blocks, block, 0)
    mean = jnp.sum(power[...], axis=0, keepdims=True) * (1.0 / half)
    level2 = 0.25 * (mean + 1e-06)
    own = [qual_ref[pl.ds(me * 4 + g, 1), :].astype(jnp.float32) for g in range(4)]

    def whiten(n):
        base = pl.multiple_of(n * 16, 16)
        reals, imags = [], []
        for g in range(4):
            cols = slice(g * 128, (g + 1) * 128)
            real = spec[pl.ds(base, 8), cols]
            imag = spec[pl.ds(base + 8, 8), cols]
            inv = lax.rsqrt(jnp.maximum(real * real + imag * imag, level2[:, cols])) * own[g]
            reals.append(real * inv)
            imags.append(imag * inv)
        value = jnp.concatenate(reals + imags, axis=0).astype(jnp.bfloat16)
        y_ref[pl.ds(pl.multiple_of(n * ROWS, ROWS), ROWS), :] = value

    first = CHUNKS[0] // GRP

    def sweep(lo, hi):
        def some(m, _):
            for v in range(5):
                whiten(lo + m * 5 + v)
            return 0

        lax.fori_loop(0, (hi - lo) // 5, some, 0)
        for n in range(hi - (hi - lo) % 5, hi):
            whiten(n)

    row = lax.broadcasted_iota(jnp.int32, (8, 128), 0)
    lane = lax.broadcasted_iota(jnp.int32, (8, 128), 1)
    hot = jnp.zeros((8, 128), jnp.float32)
    for rel, ref in enumerate((ia, ib, ic, id_)):
        for h in range(2):
            here = (row == rel * 2 + h) & (lane == ref[r + 32 * h] - r * 128)
            hot = jnp.where(here, 1.0, hot)
    hot = hot.astype(jnp.bfloat16)

    def finish(lo, hi, part_hbm, k):
        span = pl.ds(lo * ROWS, (hi - lo) * ROWS)
        copies = [
            pltpu.make_async_copy(y_ref.at[span], part_hbm, sems.at[2 * k]),
            pltpu.make_async_copy(y_ref.at[span], y_hbm.at[span], sems.at[2 * k + 1]),
        ]
        for copy in copies:
            copy.start()
        value = y_ref[lo * ROWS : hi * ROWS, :]
        picked = lax.dot_general(hot, value, (((1,), (1,)), ((), ())), preferred_element_type=jnp.float32)
        picked = picked.astype(jnp.bfloat16)
        for rel in range(4):
            out_ref = stay_ref if rel < 2 else away_ref
            out_ref[rel % 2, :, lo * ROWS : hi * ROWS] = picked[rel * 2 : rel * 2 + 2]
        return copies

    first = CHUNKS[0] // GRP
    sweep(0, first)
    copies = finish(0, first, y0_hbm, 1)
    sweep(first, ngrp)
    y_ref[ngrp * ROWS :, :] = jnp.zeros(((NGRP - ngrp) * ROWS, 128), jnp.bfloat16)
    last = (NGRP - 1) * ROWS
    y_ref[last : last + 16, :] = qual_ref[...].astype(jnp.float32).astype(jnp.bfloat16)
    copies += finish(first, NGRP, y1_hbm, 2)
    for copy in copies:
        copy.wait()


def spectra(samples, qual_t, me, lists):
    length = samples.shape[1]
    half = length // 2
    start = jnp.asarray(start_tables(length))
    vmem = pl.BlockSpec(memory_space=pltpu.VMEM)
    smem = pl.BlockSpec(memory_space=pltpu.SMEM)
    hbm = pl.BlockSpec(memory_space=pltpu.HBM)
    return pl.pallas_call(
        functools.partial(spectra_kernel, half),
        out_shape=[
            jax.ShapeDtypeStruct((CHUNKS[0] * 8, 128), jnp.bfloat16),
            jax.ShapeDtypeStruct((CHUNKS[1] * 8, 128), jnp.bfloat16),
            jax.ShapeDtypeStruct((NGRP * ROWS, 128), jnp.bfloat16),
            jax.ShapeDtypeStruct((2, 2, NGRP * ROWS), jnp.bfloat16),
            jax.ShapeDtypeStruct((2, 2, NGRP * ROWS), jnp.bfloat16),
        ],
        in_specs=[smem] * 5 + [hbm, hbm, vmem],
        out_specs=[hbm, hbm, hbm, vmem, vmem],
        scratch_shapes=[
            pltpu.VMEM((4, length, 128), jnp.bfloat16),
            pltpu.VMEM((4, 8, length), jnp.float32),
            pltpu.VMEM((NGRP * ROWS, 128), jnp.bfloat16),
            pltpu.VMEM((2, 8, length), jnp.float32),
            pltpu.VMEM((2, DBLK * 16, length), jnp.bfloat16),
            pltpu.VMEM((2 * half, 512), jnp.float32),
            pltpu.VMEM((8, 512), jnp.float32),
            pltpu.SemaphoreType.DMA((6,)),
        ],
        compiler_params=pltpu.CompilerParams(vmem_limit_bytes=63 * MB),
        cost_estimate=cost(0.001),
        name="spectra",
    )(me, *lists, samples, start, qual_t)


def join_kernel(plan, count, *refs):
    for out, row, src, at in plan:
        value = refs[src][...].reshape(-1, refs[src].shape[-1]) if at is None else refs[src][at]
        refs[count + out][row : row + value.shape[0], :] = value


def join(values, plan, shapes, name):
    vmem = pl.BlockSpec(memory_space=pltpu.VMEM)
    return pl.pallas_call(
        functools.partial(join_kernel, plan, len(values)),
        out_shape=[jax.ShapeDtypeStruct(shape, values[0].dtype) for shape in shapes],
        in_specs=[vmem] * len(values),
        out_specs=[vmem] * len(shapes),
        compiler_params=pltpu.CompilerParams(vmem_limit_bytes=16 * MB),
        cost_estimate=cost(0.001),
        name=name,
    )(*values)


def lines_kernel(pa, pb, pc, pd, *lines):
    start = 0
    for line, kc in zip(lines, CHUNKS):
        for j, piece in enumerate((pa, pb, pc, pd)):
            line[j * 16 : j * 16 + 16, :] = piece[:, start * 8 : (start + kc) * 8]
        start += kc


def split(pieces):
    vmem = pl.BlockSpec(memory_space=pltpu.VMEM)
    return pl.pallas_call(
        lines_kernel,
        out_shape=[jax.ShapeDtypeStruct((64, kc * 8), jnp.bfloat16) for kc in CHUNKS],
        in_specs=[vmem] * 4,
        out_specs=[vmem] * 2,
        compiler_params=pltpu.CompilerParams(vmem_limit_bytes=16 * MB),
        cost_estimate=cost(0.001),
        name="split",
    )(*pieces)


UNROLL = 8
HEAD = 128


def correlate_kernel(first, last, kc, offset, *refs):
    where_ref, ya, yb, yc, yd, xa, xb, xc, xd, lag_ref, qual_ref = refs[:11]
    if first:
        out_ref, ybuf, xbuf, xrow, cross, sems, table_ref, acc_ref, osem = refs[11:]
    else:
        acc_hbm, out_ref, ybuf, xbuf, xrow, cross, sems, table_ref, acc_ref, scale, stage, osem = refs[11:]
    parts = ((0, HEAD), (HEAD, kc - HEAD))
    copies = []
    for k, (lo, size) in enumerate(parts):
        span = pl.ds(lo * 8, size * 8)
        some = []
        for j, ref in enumerate((ya, yc, yb, yd)):
            rows = span if j % 2 else pl.ds((offset + lo) * 8, size * 8)
            some.append(pltpu.make_async_copy(ref.at[rows], ybuf.at[j, span], sems.at[k * 8 + j]))
        for j, ref in enumerate((xa, xb, xc, xd)):
            some.append(pltpu.make_async_copy(ref.at[:, span], xbuf.at[j, :, span], sems.at[k * 8 + 4 + j]))
        copies.append(some)
        for copy in some:
            copy.start()
    later = [pltpu.make_async_copy(lag_ref, table_ref, sems.at[16])]
    if not first:
        later.append(pltpu.make_async_copy(acc_hbm, acc_ref, sems.at[17]))

    rowid = lax.broadcasted_iota(jnp.int32, (16, 256), 0) % GRP
    lane = lax.broadcasted_iota(jnp.int32, (16, 256), 1) % GRP
    keep = rowid == lane
    zero = jnp.zeros((16, 256), jnp.bfloat16)
    stay = (lax.broadcasted_iota(jnp.int32, (8, 128), 0) < 4) == (lax.broadcasted_iota(jnp.int32, (8, 128), 1) < 64)

    def pair(n, slot):
        for far in range(4):
            for near in range(4):
                tile = xbuf[far, near * 16 : near * 16 + 16, pl.ds(pl.multiple_of(n * 128, 128), 128)].astype(jnp.float32)
                for half in range(2):
                    part = tile[half * 8 : half * 8 + 8]
                    moved = pltpu.roll(pltpu.roll(part, 4, 0), 64, 1)
                    row = (far * 4 + near) * 8
                    xrow[slot, row : row + 8, half * 128 : half * 128 + 128] = jnp.where(stay, part, moved)
        prods = []
        for a in range(2):
            tiles = []
            for p in range(0, 64, 2):
                row = (p // 4) * 8 + a * 4 + p % 4
                two = jnp.concatenate(
                    [xrow[slot, pl.ds(row, 8, stride=0), :], xrow[slot, pl.ds(row + 1, 8, stride=0), :]], axis=0
                ).astype(jnp.bfloat16)
                tiles.append(jnp.where(keep, two, zero))
            lhs = jnp.concatenate(tiles, axis=0)
            base = pl.multiple_of((2 * n + a) * ROWS, ROWS)
            reim, imre = [], []
            for s in range(SDEV):
                yr = ybuf[s, pl.ds(base, 32), :]
                yi = ybuf[s, pl.ds(base + 32, 32), :]
                reim += [yr, yi]
                imre += [-yi, yr]
            right = jnp.concatenate([jnp.concatenate(reim, axis=0), jnp.concatenate(imre, axis=0)], axis=1)
            prods.append(jnp.dot(lhs, right, preferred_element_type=jnp.float32))
        off = pl.multiple_of(n * 16, 16)
        for p in range(64):
            both = jnp.concatenate([prods[0][8 * p : 8 * p + 8], prods[1][8 * p : 8 * p + 8]], axis=0)
            both = both.astype(jnp.bfloat16)
            cross[p, pl.ds(off, 16), :] = both[:, :128]
            cross[p, pl.ds(pl.multiple_of(kc + off, 16), 16), :] = both[:, 128:]

    def pairs(m, _):
        for v in range(UNROLL):
            pair(m * UNROLL + v, v)
        return 0

    for k, ((lo, size), some) in enumerate(zip(parts, copies)):
        for copy in some:
            copy.wait()
        if k:
            for copy in later:
                copy.start()
        lax.fori_loop(lo // 16 // UNROLL, (lo + size) // 16 // UNROLL, pairs, 0)
    later[0].wait()
    table = table_ref[...]
    if last:
        flags = []
        for far in range(4):
            for near in range(4):
                flags.append(xbuf[far, near * 16 : near * 16 + 4, kc * 8 - 128 :])
        flags = jnp.concatenate([f.astype(jnp.float32) for f in flags], axis=0)[:, 64:80].astype(jnp.bfloat16)
        quality = qual_ref[...].astype(jnp.float32).astype(jnp.bfloat16)
        count = jnp.dot(flags, quality, preferred_element_type=jnp.float32)
        scale[...] = 1.0 / jnp.maximum(count, 1.0)
        later[1].wait()

    def flush(n, slot):
        return pltpu.make_async_copy(stage.at[slot], out_ref.at[:, pl.ds(pl.multiple_of(n * 8, 8), 8), :], osem.at[slot])

    def save(n):
        span = pl.ds(n * 8, 8)
        return pltpu.make_async_copy(acc_ref.at[span], out_ref.at[span], osem.at[n])

    def lags(n, _):
        spots = [where_ref[n * 8 + j] for j in range(8)]
        parts = []
        for q in range(4):
            right = jnp.concatenate([cross[spots[2 * q]], cross[spots[2 * q + 1]]], axis=1)
            prod = jnp.dot(table, right, preferred_element_type=jnp.float32)
            parts += [prod[:, :128], prod[:, 128:]]
        if last:
            slot = n % 2
            parts = [(part + acc_ref[n * 8 + j]) * scale[pl.ds(spots[j], 1), :] for j, part in enumerate(parts)]

            @pl.when(n >= 2)
            def _():
                flush(n - 2, slot).wait()

            stage[slot] = pltpu.einshape("itj->tij", jnp.stack(parts, axis=0))[:NLAG]
            flush(n, slot).start()
        else:
            for j, part in enumerate(parts):
                acc_ref[n * 8 + j] = part
            save(n).start()
        return 0

    lax.fori_loop(0, 8, lags, 0)
    if last:
        flush(6, 0).wait()
        flush(7, 1).wait()
    else:
        for n in range(8):
            save(n).wait()


def correlate(first, last, kc, offset, where, ys, xs, table, qual_t, acc=None):
    smem = pl.BlockSpec(memory_space=pltpu.SMEM)
    hbm = pl.BlockSpec(memory_space=pl.ANY)
    vmem = pl.BlockSpec(memory_space=pltpu.VMEM)
    args = (where, *ys, *xs, table, qual_t)
    in_specs = [smem] + [hbm] * 9 + [vmem]
    scratch = [
        pltpu.VMEM((4, kc * 8, 128), jnp.bfloat16),
        pltpu.VMEM((4, 64, kc * 8), jnp.bfloat16),
        pltpu.VMEM((UNROLL, 128, 256), jnp.float32),
        pltpu.VMEM((64, 2 * kc, 128), jnp.bfloat16),
        pltpu.SemaphoreType.DMA((18,)),
        pltpu.VMEM((TAU, 2 * kc), jnp.bfloat16),
        pltpu.VMEM((64, TAU, 128), jnp.float32),
    ]
    if first:
        out_shape, out_specs = (64, TAU, 128), hbm
        scratch += [pltpu.SemaphoreType.DMA((8,))]
    else:
        out_shape, out_specs = (NLAG, 64, 128), hbm
        args += (acc,)
        in_specs += [hbm]
        scratch += [
            pltpu.VMEM((64, 128), jnp.float32),
            pltpu.VMEM((2, NLAG, 8, 128), jnp.float32),
            pltpu.SemaphoreType.DMA((2,)),
        ]
    return pl.pallas_call(
        functools.partial(correlate_kernel, first, last, kc, offset),
        out_shape=jax.ShapeDtypeStruct(out_shape, jnp.float32),
        in_specs=in_specs,
        out_specs=out_specs,
        scratch_shapes=scratch,
        compiler_params=pltpu.CompilerParams(vmem_limit_bytes=60 * MB),
        cost_estimate=cost(0.001),
        name="correlate_first" if first else "correlate_last",
    )(*args)


AXES = ("zhi", "core", "y", "zlo", "x")
SIZES = (2, 2, 4, 2, 4)


def permutation(move):
    out = []
    for flat in range(128):
        at = list(np.unravel_index(flat, SIZES))
        to = move(*[int(v) for v in at])
        out.append((flat, int(np.ravel_multi_index([v % n for v, n in zip(to, SIZES)], SIZES))))
    return out


def send(value, move):
    return lax.ppermute(value, AXES, permutation(move))


def sibling(zhi, core, y, zlo, x):
    return zhi, core + 1, y, zlo, x


def across(zhi, core, y, zlo, x):
    return zhi + 1, core, y, zlo, x


def ring(phase, d):
    def move(zhi, core, y, zlo, x):
        if core == phase:
            return zhi, core, y, zlo, x + d
        return zhi, core, y + d, zlo, x

    return move


def both(zhi, core, y, zlo, x):
    return zhi + 1, core + 1, y, zlo, x


def beside(zhi, core, y, zlo, x):
    return zhi, core, y, zlo + 1, x


def aside(zhi, core, y, zlo, x):
    return zhi + 1, core, y, zlo + 1, x


def on_device(traces, src_index, quality):
    samples = jnp.transpose(traces, (1, 2, 0))
    qual_t = jnp.transpose(quality, (1, 0))
    zhi, core, yy, zlo, xx = [lax.axis_index(a) for a in AXES]
    me = zhi * 2 + core
    spot = jnp.stack([me, yy * 8 + zlo * 4 + xx])
    i = jnp.arange(64, dtype=jnp.int32)
    dx, dy = (xx - i % 4) % 4, (yy - (i // 8) % 4) % 4
    dx, dy = dx % 2 * 2 + dx // 2, dy % 2 * 2 + dy // 2
    far_step, near_step = jnp.where(core == 0, dy, dx), jnp.where(core == 0, dx, dy)
    where = far_step * 16 + near_step * 4 + jnp.bitwise_xor((i // 4) % 2, zlo) * 2 + i // 32
    table = lag_table(1000)
    tables, start = [], 0
    for kc in CHUNKS:
        tables.append(jnp.asarray(np.ascontiguousarray(table[:, :, start : start + kc]).reshape(TAU, 2 * kc)))
        start += kc

    lists = [src_index] + [send(src_index, move) for move in (sibling, across, both)]
    y0, y1, y, stay, away = spectra(samples, qual_t, spot, lists)

    out = [send(stay, beside), send(away, across), send(away, aside)]
    y0, y1, y, stay, *out = lax.optimization_barrier((y0, y1, y, stay, *out))
    far0 = send(y0, across)
    held = [stay] + out
    near = send(y, sibling)
    lanes = y.shape[0]
    both_cores = [(part, j * 2, j, part) for part in range(2) for j in range(4)]
    mine, theirs = join(held, both_cores, [(8, lanes)] * 2, "join_column")
    theirs = send(theirs, sibling)
    (got,) = join((mine, theirs), [(0, 0, 0, None), (0, 8, 1, None)], [(16, lanes)], "join_cores")
    pieces = [got] + [send(got, ring(0, d)) for d in (2, 1, 3)]
    *pieces, near = lax.optimization_barrier((*pieces, near))
    far1 = send(y1, across)
    lines = split(pieces)
    xs0 = [lines[0]] + [send(lines[0], ring(1, d)) for d in (2, 1, 3)]
    *xs0, line1 = lax.optimization_barrier((*xs0, lines[1]))
    xs1 = [line1] + [send(line1, ring(1, d)) for d in (2, 1, 3)]
    acc = correlate(
        True, False, CHUNKS[0], 0, where, (y, near, far0, send(far0, sibling)), xs0, tables[0], qual_t
    )
    far1, acc, *xs1 = lax.optimization_barrier((far1, acc, *xs1))
    out = correlate(
        False, True, CHUNKS[1], CHUNKS[0], where, (y, near, far1, send(far1, sibling)), xs1, tables[1], qual_t, acc
    )
    return jnp.transpose(out, (1, 0, 2))


def solution(mesh):
    fine = Mesh(mesh.devices.reshape(2, 2, 4, 2, 4), ("zhi", "core", "y", "zlo", "x"))
    rcv = ("y", "zlo", "x")
    src = ("zhi", "core")
    return jax.shard_map(
        on_device,
        mesh=fine,
        in_specs=(P(rcv, src, None), P(src), P(rcv, None)),
        out_specs=P(src, None, rcv),
        check_vma=False,
    )
```

```python
import functools
import math

import jax
import jax.numpy as jnp
import ml_dtypes
import numpy as np
from jax import lax
from jax.experimental import pallas as pl
from jax.experimental.pallas import tpu as pltpu
from jax.sharding import Mesh, PartitionSpec as P

LAGH = 100
NLAG = 2 * LAGH + 1
TAU = 208
GRP = 8
KPAD = 1024
NGRP = KPAD // GRP
SDEV = 4
ROWS = 64
MB = 1 << 20


def start_tables(length):
    bins = np.arange(1, GRP + 1, dtype=np.float64)
    times = np.arange(length, dtype=np.float64)
    phase = 2.0 * math.pi / length * ((bins[:, None] * times[None, :]) % length)
    step = 2.0 * math.pi / length * ((GRP * times) % length)
    step = np.broadcast_to(step[None, :], phase.shape)
    return np.stack([np.cos(phase), -np.sin(phase), np.cos(step), np.sin(step)]).astype(np.float32)


def lag_table(half):
    bins = np.arange(1, half + 1, dtype=np.int64)
    lags = np.arange(-LAGH, LAGH + 1, dtype=np.int64)
    phase = 2.0 * math.pi / (2 * half) * ((lags[:, None] * bins[None, :]) % (2 * half))
    weight = np.where(bins == half, 1.0, 2.0)[None, :] / math.sqrt(half)
    out = np.zeros((TAU, 2, KPAD), np.float32)
    out[:NLAG, 0, :half] = weight * np.cos(phase)
    out[:NLAG, 1, :half] = -weight * np.sin(phase)
    return out.astype(ml_dtypes.bfloat16)


def cost(us):
    return pl.CostEstimate(flops=int(us * 1.1e9), transcendentals=0, bytes_accessed=1024)


DBLK = 25
CHUNKS = (448, 576)


def spectra_kernel(
    half, me_ref, ia, ib, ic, id_, x_hbm, start_hbm, qual_ref, y0_hbm, y1_hbm, y_hbm, stay_ref, away_ref,
    x_ref, start_ref, y_ref, state, table, spec, power, sems,
):
    ngrp = half // GRP
    length = 2 * half
    blocks = ngrp // DBLK
    me, r = me_ref[0], me_ref[1]
    load_start = pltpu.make_async_copy(start_hbm, start_ref, sems.at[0])
    load_start.start()
    load = pltpu.make_async_copy(x_hbm, x_ref, sems.at[1])
    load.start()
    load_start.wait()

    def gen(slot):
        for lo in range(0, length, 128):
            cols = slice(lo, min(lo + 128, length))
            cos, sin = state[0, :, cols], state[1, :, cols]
            rc, rs = start_ref[2, :, cols], start_ref[3, :, cols]
            for n in range(DBLK):
                table[slot, n * 16 : n * 16 + 16, cols] = jnp.concatenate([cos, sin], axis=0).astype(jnp.bfloat16)
                cos, sin = cos * rc + sin * rs, sin * rc - cos * rs
            state[0, :, cols] = cos
            state[1, :, cols] = sin

    state[0] = start_ref[0]
    state[1] = start_ref[1]
    power[...] = jnp.zeros_like(power)
    gen(0)
    load.wait()
    samples = jnp.concatenate([x_ref[g] for g in range(4)], axis=1)

    def block(b, _):
        slot = b % 2
        prod = jnp.dot(table[slot], samples, preferred_element_type=jnp.float32)
        gen(1 - slot)
        spec[pl.ds(pl.multiple_of(b * (DBLK * 16), DBLK * 16), DBLK * 16), :] = prod
        power[...] += jnp.sum((prod * prod).reshape(DBLK * 2, 8, 512), axis=0)
        return 0

    lax.fori_loop(0, blocks, block, 0)
    mean = jnp.sum(power[...], axis=0, keepdims=True) * (1.0 / half)
    level2 = 0.25 * (mean + 1e-06)
    own = [qual_ref[pl.ds(me * 4 + g, 1), :].astype(jnp.float32) for g in range(4)]

    def whiten(n):
        base = pl.multiple_of(n * 16, 16)
        reals, imags = [], []
        for g in range(4):
            cols = slice(g * 128, (g + 1) * 128)
            real = spec[pl.ds(base, 8), cols]
            imag = spec[pl.ds(base + 8, 8), cols]
            inv = lax.rsqrt(jnp.maximum(real * real + imag * imag, level2[:, cols])) * own[g]
            reals.append(real * inv)
            imags.append(imag * inv)
        value = jnp.concatenate(reals + imags, axis=0).astype(jnp.bfloat16)
        y_ref[pl.ds(pl.multiple_of(n * ROWS, ROWS), ROWS), :] = value

    first = CHUNKS[0] // GRP

    def sweep(lo, hi):
        def some(m, _):
            for v in range(5):
                whiten(lo + m * 5 + v)
            return 0

        lax.fori_loop(0, (hi - lo) // 5, some, 0)
        for n in range(hi - (hi - lo) % 5, hi):
            whiten(n)

    row = lax.broadcasted_iota(jnp.int32, (8, 128), 0)
    lane = lax.broadcasted_iota(jnp.int32, (8, 128), 1)
    hot = jnp.zeros((8, 128), jnp.float32)
    for rel, ref in enumerate((ia, ib, ic, id_)):
        for h in range(2):
            here = (row == rel * 2 + h) & (lane == ref[r + 32 * h] - r * 128)
            hot = jnp.where(here, 1.0, hot)
    hot = hot.astype(jnp.bfloat16)

    def finish(lo, hi, part_hbm, k):
        span = pl.ds(lo * ROWS, (hi - lo) * ROWS)
        copies = [
            pltpu.make_async_copy(y_ref.at[span], part_hbm, sems.at[2 * k]),
            pltpu.make_async_copy(y_ref.at[span], y_hbm.at[span], sems.at[2 * k + 1]),
        ]
        for copy in copies:
            copy.start()
        value = y_ref[lo * ROWS : hi * ROWS, :]
        picked = lax.dot_general(hot, value, (((1,), (1,)), ((), ())), preferred_element_type=jnp.float32)
        picked = picked.astype(jnp.bfloat16)
        for rel in range(4):
            out_ref = stay_ref if rel < 2 else away_ref
            out_ref[rel % 2, :, lo * ROWS : hi * ROWS] = picked[rel * 2 : rel * 2 + 2]
        return copies

    first = CHUNKS[0] // GRP
    sweep(0, first)
    copies = finish(0, first, y0_hbm, 1)
    sweep(first, ngrp)
    y_ref[ngrp * ROWS :, :] = jnp.zeros(((NGRP - ngrp) * ROWS, 128), jnp.bfloat16)
    last = (NGRP - 1) * ROWS
    y_ref[last : last + 16, :] = qual_ref[...].astype(jnp.float32).astype(jnp.bfloat16)
    copies += finish(first, NGRP, y1_hbm, 2)
    for copy in copies:
        copy.wait()


def spectra(samples, qual_t, me, lists):
    length = samples.shape[1]
    half = length // 2
    start = jnp.asarray(start_tables(length))
    vmem = pl.BlockSpec(memory_space=pltpu.VMEM)
    smem = pl.BlockSpec(memory_space=pltpu.SMEM)
    hbm = pl.BlockSpec(memory_space=pltpu.HBM)
    return pl.pallas_call(
        functools.partial(spectra_kernel, half),
        out_shape=[
            jax.ShapeDtypeStruct((CHUNKS[0] * 8, 128), jnp.bfloat16),
            jax.ShapeDtypeStruct((CHUNKS[1] * 8, 128), jnp.bfloat16),
            jax.ShapeDtypeStruct((NGRP * ROWS, 128), jnp.bfloat16),
            jax.ShapeDtypeStruct((2, 2, NGRP * ROWS), jnp.bfloat16),
            jax.ShapeDtypeStruct((2, 2, NGRP * ROWS), jnp.bfloat16),
        ],
        in_specs=[smem] * 5 + [hbm, hbm, vmem],
        out_specs=[hbm, hbm, hbm, vmem, vmem],
        scratch_shapes=[
            pltpu.VMEM((4, length, 128), jnp.bfloat16),
            pltpu.VMEM((4, 8, length), jnp.float32),
            pltpu.VMEM((NGRP * ROWS, 128), jnp.bfloat16),
            pltpu.VMEM((2, 8, length), jnp.float32),
            pltpu.VMEM((2, DBLK * 16, length), jnp.bfloat16),
            pltpu.VMEM((2 * half, 512), jnp.float32),
            pltpu.VMEM((8, 512), jnp.float32),
            pltpu.SemaphoreType.DMA((6,)),
        ],
        compiler_params=pltpu.CompilerParams(vmem_limit_bytes=63 * MB),
        cost_estimate=cost(0.001),
        name="spectra",
    )(me, *lists, samples, start, qual_t)


def join_kernel(plan, count, *refs):
    for out, row, src, at in plan:
        value = refs[src][...].reshape(-1, refs[src].shape[-1]) if at is None else refs[src][at]
        refs[count + out][row : row + value.shape[0], :] = value


def join(values, plan, shapes, name):
    vmem = pl.BlockSpec(memory_space=pltpu.VMEM)
    return pl.pallas_call(
        functools.partial(join_kernel, plan, len(values)),
        out_shape=[jax.ShapeDtypeStruct(shape, values[0].dtype) for shape in shapes],
        in_specs=[vmem] * len(values),
        out_specs=[vmem] * len(shapes),
        compiler_params=pltpu.CompilerParams(vmem_limit_bytes=16 * MB),
        cost_estimate=cost(0.001),
        name=name,
    )(*values)


def lines_kernel(pa, pb, pc, pd, *lines):
    start = 0
    for line, kc in zip(lines, CHUNKS):
        for j, piece in enumerate((pa, pb, pc, pd)):
            line[j * 16 : j * 16 + 16, :] = piece[:, start * 8 : (start + kc) * 8]
        start += kc


def split(pieces):
    vmem = pl.BlockSpec(memory_space=pltpu.VMEM)
    return pl.pallas_call(
        lines_kernel,
        out_shape=[jax.ShapeDtypeStruct((64, kc * 8), jnp.bfloat16) for kc in CHUNKS],
        in_specs=[vmem] * 4,
        out_specs=[vmem] * 2,
        compiler_params=pltpu.CompilerParams(vmem_limit_bytes=16 * MB),
        cost_estimate=cost(0.001),
        name="split",
    )(*pieces)


UNROLL = 8
HEAD = 64


def correlate_kernel(first, last, kc, offset, *refs):
    where_ref, ya, yb, yc, yd, xa, xb, xc, xd, lag_ref, qual_ref = refs[:11]
    if first:
        out_ref, ybuf, xbuf, xrow, cross, sems, table_ref, acc_ref, osem = refs[11:]
    else:
        acc_hbm, out_ref, ybuf, xbuf, xrow, cross, sems, table_ref, acc_ref, scale, stage, osem = refs[11:]
    parts = ((0, HEAD), (HEAD, kc - HEAD))
    copies = []
    for k, (lo, size) in enumerate(parts):
        span = pl.ds(lo * 8, size * 8)
        some = []
        for j, ref in enumerate((ya, yc, yb, yd)):
            rows = span if j % 2 else pl.ds((offset + lo) * 8, size * 8)
            some.append(pltpu.make_async_copy(ref.at[rows], ybuf.at[j, span], sems.at[k * 8 + j]))
        for j, ref in enumerate((xa, xb, xc, xd)):
            some.append(pltpu.make_async_copy(ref.at[:, span], xbuf.at[j, :, span], sems.at[k * 8 + 4 + j]))
        copies.append(some)
        for copy in some:
            copy.start()
    later = [pltpu.make_async_copy(lag_ref, table_ref, sems.at[16])]
    if not first:
        later.append(pltpu.make_async_copy(acc_hbm, acc_ref, sems.at[17]))

    rowid = lax.broadcasted_iota(jnp.int32, (16, 256), 0) % GRP
    lane = lax.broadcasted_iota(jnp.int32, (16, 256), 1) % GRP
    keep = rowid == lane
    zero = jnp.zeros((16, 256), jnp.bfloat16)
    stay = (lax.broadcasted_iota(jnp.int32, (8, 128), 0) < 4) == (lax.broadcasted_iota(jnp.int32, (8, 128), 1) < 64)

    def pair(n, slot):
        for far in range(4):
            for near in range(4):
                tile = xbuf[far, near * 16 : near * 16 + 16, pl.ds(pl.multiple_of(n * 128, 128), 128)].astype(jnp.float32)
                for half in range(2):
                    part = tile[half * 8 : half * 8 + 8]
                    moved = pltpu.roll(pltpu.roll(part, 4, 0), 64, 1)
                    row = (far * 4 + near) * 8
                    xrow[slot, row : row + 8, half * 128 : half * 128 + 128] = jnp.where(stay, part, moved)
        prods = []
        for a in range(2):
            tiles = []
            for p in range(0, 64, 2):
                row = (p // 4) * 8 + a * 4 + p % 4
                two = jnp.concatenate(
                    [xrow[slot, pl.ds(row, 8, stride=0), :], xrow[slot, pl.ds(row + 1, 8, stride=0), :]], axis=0
                ).astype(jnp.bfloat16)
                tiles.append(jnp.where(keep, two, zero))
            lhs = jnp.concatenate(tiles, axis=0)
            base = pl.multiple_of((2 * n + a) * ROWS, ROWS)
            reim, imre = [], []
            for s in range(SDEV):
                yr = ybuf[s, pl.ds(base, 32), :]
                yi = ybuf[s, pl.ds(base + 32, 32), :]
                reim += [yr, yi]
                imre += [-yi, yr]
            right = jnp.concatenate([jnp.concatenate(reim, axis=0), jnp.concatenate(imre, axis=0)], axis=1)
            prods.append(jnp.dot(lhs, right, preferred_element_type=jnp.float32))
        off = pl.multiple_of(n * 16, 16)
        for p in range(64):
            both = jnp.concatenate([prods[0][8 * p : 8 * p + 8], prods[1][8 * p : 8 * p + 8]], axis=0)
            both = both.astype(jnp.bfloat16)
            cross[p, pl.ds(off, 16), :] = both[:, :128]
            cross[p, pl.ds(pl.multiple_of(kc + off, 16), 16), :] = both[:, 128:]

    def pairs(m, _):
        for v in range(UNROLL):
            pair(HEAD // 16 + m * UNROLL + v, v)
        return 0

    for k, ((lo, size), some) in enumerate(zip(parts, copies)):
        for copy in some:
            copy.wait()
        if k:
            for copy in later:
                copy.start()
        if k:
            lax.fori_loop(0, size // 16 // UNROLL, pairs, 0)
        else:
            for v in range(HEAD // 16):
                pair(v, v)
    later[0].wait()
    table = table_ref[...]
    if last:
        flags = []
        for far in range(4):
            for near in range(4):
                flags.append(xbuf[far, near * 16 : near * 16 + 4, kc * 8 - 128 :])
        flags = jnp.concatenate([f.astype(jnp.float32) for f in flags], axis=0)[:, 64:80].astype(jnp.bfloat16)
        quality = qual_ref[...].astype(jnp.float32).astype(jnp.bfloat16)
        count = jnp.dot(flags, quality, preferred_element_type=jnp.float32)
        scale[...] = 1.0 / jnp.maximum(count, 1.0)
        later[1].wait()

    def flush(n, slot):
        return pltpu.make_async_copy(stage.at[slot], out_ref.at[:, pl.ds(pl.multiple_of(n * 8, 8), 8), :], osem.at[slot])

    def save(n):
        span = pl.ds(n * 8, 8)
        return pltpu.make_async_copy(acc_ref.at[span], out_ref.at[span], osem.at[n])

    def lags(n, _):
        spots = [where_ref[n * 8 + j] for j in range(8)]
        parts = []
        for q in range(4):
            right = jnp.concatenate([cross[spots[2 * q]], cross[spots[2 * q + 1]]], axis=1)
            prod = jnp.dot(table, right, preferred_element_type=jnp.float32)
            parts += [prod[:, :128], prod[:, 128:]]
        if last:
            slot = n % 2
            parts = [(part + acc_ref[n * 8 + j]) * scale[pl.ds(spots[j], 1), :] for j, part in enumerate(parts)]

            @pl.when(n >= 2)
            def _():
                flush(n - 2, slot).wait()

            stage[slot] = pltpu.einshape("itj->tij", jnp.stack(parts, axis=0))[:NLAG]
            flush(n, slot).start()
        else:
            for j, part in enumerate(parts):
                acc_ref[n * 8 + j] = part
            save(n).start()
        return 0

    lax.fori_loop(0, 8, lags, 0)
    if last:
        flush(6, 0).wait()
        flush(7, 1).wait()
    else:
        for n in range(8):
            save(n).wait()


def correlate(first, last, kc, offset, where, ys, xs, table, qual_t, acc=None):
    smem = pl.BlockSpec(memory_space=pltpu.SMEM)
    hbm = pl.BlockSpec(memory_space=pl.ANY)
    vmem = pl.BlockSpec(memory_space=pltpu.VMEM)
    args = (where, *ys, *xs, table, qual_t)
    in_specs = [smem] + [hbm] * 9 + [vmem]
    scratch = [
        pltpu.VMEM((4, kc * 8, 128), jnp.bfloat16),
        pltpu.VMEM((4, 64, kc * 8), jnp.bfloat16),
        pltpu.VMEM((UNROLL, 128, 256), jnp.float32),
        pltpu.VMEM((64, 2 * kc, 128), jnp.bfloat16),
        pltpu.SemaphoreType.DMA((18,)),
        pltpu.VMEM((TAU, 2 * kc), jnp.bfloat16),
        pltpu.VMEM((64, TAU, 128), jnp.float32),
    ]
    if first:
        out_shape, out_specs = (64, TAU, 128), hbm
        scratch += [pltpu.SemaphoreType.DMA((8,))]
    else:
        out_shape, out_specs = (NLAG, 64, 128), hbm
        args += (acc,)
        in_specs += [hbm]
        scratch += [
            pltpu.VMEM((64, 128), jnp.float32),
            pltpu.VMEM((2, NLAG, 8, 128), jnp.float32),
            pltpu.SemaphoreType.DMA((2,)),
        ]
    return pl.pallas_call(
        functools.partial(correlate_kernel, first, last, kc, offset),
        out_shape=jax.ShapeDtypeStruct(out_shape, jnp.float32),
        in_specs=in_specs,
        out_specs=out_specs,
        scratch_shapes=scratch,
        compiler_params=pltpu.CompilerParams(vmem_limit_bytes=60 * MB),
        cost_estimate=cost(0.001),
        name="correlate_first" if first else "correlate_last",
    )(*args)


AXES = ("zhi", "core", "y", "zlo", "x")
SIZES = (2, 2, 4, 2, 4)


def permutation(move):
    out = []
    for flat in range(128):
        at = list(np.unravel_index(flat, SIZES))
        to = move(*[int(v) for v in at])
        out.append((flat, int(np.ravel_multi_index([v % n for v, n in zip(to, SIZES)], SIZES))))
    return out


def send(value, move):
    return lax.ppermute(value, AXES, permutation(move))


def sibling(zhi, core, y, zlo, x):
    return zhi, core + 1, y, zlo, x


def across(zhi, core, y, zlo, x):
    return zhi + 1, core, y, zlo, x


def ring(phase, d):
    def move(zhi, core, y, zlo, x):
        if core == phase:
            return zhi, core, y, zlo, x + d
        return zhi, core, y + d, zlo, x

    return move


def both(zhi, core, y, zlo, x):
    return zhi + 1, core + 1, y, zlo, x


def beside(zhi, core, y, zlo, x):
    return zhi, core, y, zlo + 1, x


def aside(zhi, core, y, zlo, x):
    return zhi + 1, core, y, zlo + 1, x


def on_device(traces, src_index, quality):
    samples = jnp.transpose(traces, (1, 2, 0))
    qual_t = jnp.transpose(quality, (1, 0))
    zhi, core, yy, zlo, xx = [lax.axis_index(a) for a in AXES]
    me = zhi * 2 + core
    spot = jnp.stack([me, yy * 8 + zlo * 4 + xx])
    i = jnp.arange(64, dtype=jnp.int32)
    dx, dy = (xx - i % 4) % 4, (yy - (i // 8) % 4) % 4
    dx, dy = dx % 2 * 2 + dx // 2, dy % 2 * 2 + dy // 2
    far_step, near_step = jnp.where(core == 0, dy, dx), jnp.where(core == 0, dx, dy)
    where = far_step * 16 + near_step * 4 + jnp.bitwise_xor((i // 4) % 2, zlo) * 2 + i // 32
    table = lag_table(1000)
    tables, start = [], 0
    for kc in CHUNKS:
        tables.append(jnp.asarray(np.ascontiguousarray(table[:, :, start : start + kc]).reshape(TAU, 2 * kc)))
        start += kc

    lists = [src_index] + [send(src_index, move) for move in (sibling, across, both)]
    y0, y1, y, stay, away = spectra(samples, qual_t, spot, lists)

    out = [send(stay, beside), send(away, across), send(away, aside)]
    y0, y1, y, stay, *out = lax.optimization_barrier((y0, y1, y, stay, *out))
    far0 = send(y0, across)
    held = [stay] + out
    near = send(y, sibling)
    lanes = y.shape[0]
    both_cores = [(part, j * 2, j, part) for part in range(2) for j in range(4)]
    mine, theirs = join(held, both_cores, [(8, lanes)] * 2, "join_column")
    theirs = send(theirs, sibling)
    (got,) = join((mine, theirs), [(0, 0, 0, None), (0, 8, 1, None)], [(16, lanes)], "join_cores")
    pieces = [got] + [send(got, ring(0, d)) for d in (2, 1, 3)]
    *pieces, near = lax.optimization_barrier((*pieces, near))
    far1 = send(y1, across)
    lines = split(pieces)
    xs0 = [lines[0]] + [send(lines[0], ring(1, d)) for d in (2, 1, 3)]
    *xs0, line1 = lax.optimization_barrier((*xs0, lines[1]))
    xs1 = [line1] + [send(line1, ring(1, d)) for d in (2, 1, 3)]
    acc = correlate(
        True, False, CHUNKS[0], 0, where, (y, near, far0, send(far0, sibling)), xs0, tables[0], qual_t
    )
    far1, acc, *xs1 = lax.optimization_barrier((far1, acc, *xs1))
    out = correlate(
        False, True, CHUNKS[1], CHUNKS[0], where, (y, near, far1, send(far1, sibling)), xs1, tables[1], qual_t, acc
    )
    return jnp.transpose(out, (1, 0, 2))


def solution(mesh):
    fine = Mesh(mesh.devices.reshape(2, 2, 4, 2, 4), ("zhi", "core", "y", "zlo", "x"))
    rcv = ("y", "zlo", "x")
    src = ("zhi", "core")
    return jax.shard_map(
        on_device,
        mesh=fine,
        in_specs=(P(rcv, src, None), P(src), P(rcv, None)),
        out_specs=P(src, None, rcv),
        check_vma=False,
    )
```

```python
import functools
import math

import jax
import jax.numpy as jnp
import ml_dtypes
import numpy as np
from jax import lax
from jax.experimental import pallas as pl
from jax.experimental.pallas import tpu as pltpu
from jax.sharding import Mesh, PartitionSpec as P

LAGH = 100
NLAG = 2 * LAGH + 1
TAU = 208
GRP = 8
KPAD = 1024
NGRP = KPAD // GRP
SDEV = 4
ROWS = 64
MB = 1 << 20


def start_tables(length):
    bins = np.arange(1, GRP + 1, dtype=np.float64)
    times = np.arange(length, dtype=np.float64)
    phase = 2.0 * math.pi / length * ((bins[:, None] * times[None, :]) % length)
    step = 2.0 * math.pi / length * ((GRP * times) % length)
    step = np.broadcast_to(step[None, :], phase.shape)
    return np.stack([np.cos(phase), -np.sin(phase), np.cos(step), np.sin(step)]).astype(np.float32)


def lag_table(half):
    bins = np.arange(1, half + 1, dtype=np.int64)
    lags = np.arange(-LAGH, LAGH + 1, dtype=np.int64)
    phase = 2.0 * math.pi / (2 * half) * ((lags[:, None] * bins[None, :]) % (2 * half))
    weight = np.where(bins == half, 1.0, 2.0)[None, :] / math.sqrt(half)
    out = np.zeros((TAU, 2, KPAD), np.float32)
    out[:NLAG, 0, :half] = weight * np.cos(phase)
    out[:NLAG, 1, :half] = -weight * np.sin(phase)
    return out.astype(ml_dtypes.bfloat16)


def cost(us):
    return pl.CostEstimate(flops=int(us * 1.1e9), transcendentals=0, bytes_accessed=1024)


DBLK = 25
CHUNKS = (448, 576)


def spectra_kernel(
    half, me_ref, ia, ib, ic, id_, x_hbm, start_hbm, qual_ref, y0_hbm, y1_hbm, y_hbm, stay_ref, away_ref,
    x_ref, start_ref, y_ref, state, table, spec, power, sems,
):
    ngrp = half // GRP
    length = 2 * half
    blocks = ngrp // DBLK
    me, r = me_ref[0], me_ref[1]
    load_start = pltpu.make_async_copy(start_hbm, start_ref, sems.at[0])
    load_start.start()
    load = pltpu.make_async_copy(x_hbm, x_ref, sems.at[1])
    load.start()
    load_start.wait()

    def gen(slot):
        for lo in range(0, length, 128):
            cols = slice(lo, min(lo + 128, length))
            cos, sin = state[0, :, cols], state[1, :, cols]
            rc, rs = start_ref[2, :, cols], start_ref[3, :, cols]
            for n in range(DBLK):
                table[slot, n * 16 : n * 16 + 16, cols] = jnp.concatenate([cos, sin], axis=0).astype(jnp.bfloat16)
                cos, sin = cos * rc + sin * rs, sin * rc - cos * rs
            state[0, :, cols] = cos
            state[1, :, cols] = sin

    state[0] = start_ref[0]
    state[1] = start_ref[1]
    power[...] = jnp.zeros_like(power)
    gen(0)
    load.wait()
    samples = jnp.concatenate([x_ref[g] for g in range(4)], axis=1)

    def block(b, _):
        slot = b % 2
        prod = jnp.dot(table[slot], samples, preferred_element_type=jnp.float32)
        gen(1 - slot)
        spec[pl.ds(pl.multiple_of(b * (DBLK * 16), DBLK * 16), DBLK * 16), :] = prod
        power[...] += jnp.sum((prod * prod).reshape(DBLK * 2, 8, 512), axis=0)
        return 0

    lax.fori_loop(0, blocks, block, 0)
    mean = jnp.sum(power[...], axis=0, keepdims=True) * (1.0 / half)
    level2 = 0.25 * (mean + 1e-06)
    own = [qual_ref[pl.ds(me * 4 + g, 1), :].astype(jnp.float32) for g in range(4)]

    def whiten(n):
        base = pl.multiple_of(n * 16, 16)
        reals, imags = [], []
        for g in range(4):
            cols = slice(g * 128, (g + 1) * 128)
            real = spec[pl.ds(base, 8), cols]
            imag = spec[pl.ds(base + 8, 8), cols]
            inv = lax.rsqrt(jnp.maximum(real * real + imag * imag, level2[:, cols])) * own[g]
            reals.append(real * inv)
            imags.append(imag * inv)
        value = jnp.concatenate(reals + imags, axis=0).astype(jnp.bfloat16)
        y_ref[pl.ds(pl.multiple_of(n * ROWS, ROWS), ROWS), :] = value

    first = CHUNKS[0] // GRP

    def sweep(lo, hi):
        def some(m, _):
            for v in range(5):
                whiten(lo + m * 5 + v)
            return 0

        lax.fori_loop(0, (hi - lo) // 5, some, 0)
        for n in range(hi - (hi - lo) % 5, hi):
            whiten(n)

    row = lax.broadcasted_iota(jnp.int32, (8, 128), 0)
    lane = lax.broadcasted_iota(jnp.int32, (8, 128), 1)
    hot = jnp.zeros((8, 128), jnp.float32)
    for rel, ref in enumerate((ia, ib, ic, id_)):
        for h in range(2):
            here = (row == rel * 2 + h) & (lane == ref[r + 32 * h] - r * 128)
            hot = jnp.where(here, 1.0, hot)
    hot = hot.astype(jnp.bfloat16)

    def finish(lo, hi, part_hbm, k):
        span = pl.ds(lo * ROWS, (hi - lo) * ROWS)
        copies = [
            pltpu.make_async_copy(y_ref.at[span], part_hbm, sems.at[2 * k]),
            pltpu.make_async_copy(y_ref.at[span], y_hbm.at[span], sems.at[2 * k + 1]),
        ]
        for copy in copies:
            copy.start()
        value = y_ref[lo * ROWS : hi * ROWS, :]
        picked = lax.dot_general(hot, value, (((1,), (1,)), ((), ())), preferred_element_type=jnp.float32)
        picked = picked.astype(jnp.bfloat16)
        for rel in range(4):
            out_ref = stay_ref if rel < 2 else away_ref
            out_ref[rel % 2, :, lo * ROWS : hi * ROWS] = picked[rel * 2 : rel * 2 + 2]
        return copies

    first = CHUNKS[0] // GRP
    sweep(0, first)
    copies = finish(0, first, y0_hbm, 1)
    sweep(first, ngrp)
    y_ref[ngrp * ROWS :, :] = jnp.zeros(((NGRP - ngrp) * ROWS, 128), jnp.bfloat16)
    last = (NGRP - 1) * ROWS
    y_ref[last : last + 16, :] = qual_ref[...].astype(jnp.float32).astype(jnp.bfloat16)
    copies += finish(first, NGRP, y1_hbm, 2)
    for copy in copies:
        copy.wait()


def spectra(samples, qual_t, me, lists):
    length = samples.shape[1]
    half = length // 2
    start = jnp.asarray(start_tables(length))
    vmem = pl.BlockSpec(memory_space=pltpu.VMEM)
    smem = pl.BlockSpec(memory_space=pltpu.SMEM)
    hbm = pl.BlockSpec(memory_space=pltpu.HBM)
    return pl.pallas_call(
        functools.partial(spectra_kernel, half),
        out_shape=[
            jax.ShapeDtypeStruct((CHUNKS[0] * 8, 128), jnp.bfloat16),
            jax.ShapeDtypeStruct((CHUNKS[1] * 8, 128), jnp.bfloat16),
            jax.ShapeDtypeStruct((NGRP * ROWS, 128), jnp.bfloat16),
            jax.ShapeDtypeStruct((2, 2, NGRP * ROWS), jnp.bfloat16),
            jax.ShapeDtypeStruct((2, 2, NGRP * ROWS), jnp.bfloat16),
        ],
        in_specs=[smem] * 5 + [hbm, hbm, vmem],
        out_specs=[hbm, hbm, hbm, vmem, vmem],
        scratch_shapes=[
            pltpu.VMEM((4, length, 128), jnp.bfloat16),
            pltpu.VMEM((4, 8, length), jnp.float32),
            pltpu.VMEM((NGRP * ROWS, 128), jnp.bfloat16),
            pltpu.VMEM((2, 8, length), jnp.float32),
            pltpu.VMEM((2, DBLK * 16, length), jnp.bfloat16),
            pltpu.VMEM((2 * half, 512), jnp.float32),
            pltpu.VMEM((8, 512), jnp.float32),
            pltpu.SemaphoreType.DMA((6,)),
        ],
        compiler_params=pltpu.CompilerParams(vmem_limit_bytes=63 * MB),
        cost_estimate=cost(0.001),
        name="spectra",
    )(me, *lists, samples, start, qual_t)


def join_kernel(plan, count, *refs):
    for out, row, src, at in plan:
        value = refs[src][...].reshape(-1, refs[src].shape[-1]) if at is None else refs[src][at]
        refs[count + out][row : row + value.shape[0], :] = value


def join(values, plan, shapes, name):
    vmem = pl.BlockSpec(memory_space=pltpu.VMEM)
    return pl.pallas_call(
        functools.partial(join_kernel, plan, len(values)),
        out_shape=[jax.ShapeDtypeStruct(shape, values[0].dtype) for shape in shapes],
        in_specs=[vmem] * len(values),
        out_specs=[vmem] * len(shapes),
        compiler_params=pltpu.CompilerParams(vmem_limit_bytes=16 * MB),
        cost_estimate=cost(0.001),
        name=name,
    )(*values)


def lines_kernel(pa, pb, pc, pd, *lines):
    start = 0
    for line, kc in zip(lines, CHUNKS):
        for j, piece in enumerate((pa, pb, pc, pd)):
            line[j * 16 : j * 16 + 16, :] = piece[:, start * 8 : (start + kc) * 8]
        start += kc


def split(pieces):
    vmem = pl.BlockSpec(memory_space=pltpu.VMEM)
    return pl.pallas_call(
        lines_kernel,
        out_shape=[jax.ShapeDtypeStruct((64, kc * 8), jnp.bfloat16) for kc in CHUNKS],
        in_specs=[vmem] * 4,
        out_specs=[vmem] * 2,
        compiler_params=pltpu.CompilerParams(vmem_limit_bytes=16 * MB),
        cost_estimate=cost(0.001),
        name="split",
    )(*pieces)


UNROLL = 8
HEAD = 64


def correlate_kernel(first, last, kc, offset, *refs):
    where_ref, ya, yb, yc, yd, xa, xb, xc, xd, lag_ref, qual_ref = refs[:11]
    if first:
        out_ref, ybuf, xbuf, xrow, cross, sems, table_ref, acc_ref, osem = refs[11:]
    else:
        acc_hbm, out_ref, ybuf, xbuf, xrow, cross, sems, table_ref, acc_ref, scale, stage, osem = refs[11:]
    parts = ((0, HEAD), (HEAD, 128), (HEAD + 128, kc - HEAD - 128))
    copies = []
    for k, (lo, size) in enumerate(parts):
        span = pl.ds(lo * 8, size * 8)
        some = []
        for j, ref in enumerate((ya, yc, yb, yd)):
            rows = span if j % 2 else pl.ds((offset + lo) * 8, size * 8)
            some.append(pltpu.make_async_copy(ref.at[rows], ybuf.at[j, span], sems.at[k * 8 + j]))
        for j, ref in enumerate((xa, xb, xc, xd)):
            some.append(pltpu.make_async_copy(ref.at[:, span], xbuf.at[j, :, span], sems.at[k * 8 + 4 + j]))
        copies.append(some)
        for copy in some:
            copy.start()
    later = [pltpu.make_async_copy(lag_ref, table_ref, sems.at[24])]
    if not first:
        later.append(pltpu.make_async_copy(acc_hbm, acc_ref, sems.at[25]))

    rowid = lax.broadcasted_iota(jnp.int32, (16, 256), 0) % GRP
    lane = lax.broadcasted_iota(jnp.int32, (16, 256), 1) % GRP
    keep = rowid == lane
    zero = jnp.zeros((16, 256), jnp.bfloat16)
    stay = (lax.broadcasted_iota(jnp.int32, (8, 128), 0) < 4) == (lax.broadcasted_iota(jnp.int32, (8, 128), 1) < 64)

    def pair(n, slot):
        for far in range(4):
            for near in range(4):
                tile = xbuf[far, near * 16 : near * 16 + 16, pl.ds(pl.multiple_of(n * 128, 128), 128)].astype(jnp.float32)
                for half in range(2):
                    part = tile[half * 8 : half * 8 + 8]
                    moved = pltpu.roll(pltpu.roll(part, 4, 0), 64, 1)
                    row = (far * 4 + near) * 8
                    xrow[slot, row : row + 8, half * 128 : half * 128 + 128] = jnp.where(stay, part, moved)
        prods = []
        for a in range(2):
            tiles = []
            for p in range(0, 64, 2):
                row = (p // 4) * 8 + a * 4 + p % 4
                two = jnp.concatenate(
                    [xrow[slot, pl.ds(row, 8, stride=0), :], xrow[slot, pl.ds(row + 1, 8, stride=0), :]], axis=0
                ).astype(jnp.bfloat16)
                tiles.append(jnp.where(keep, two, zero))
            lhs = jnp.concatenate(tiles, axis=0)
            base = pl.multiple_of((2 * n + a) * ROWS, ROWS)
            reim, imre = [], []
            for s in range(SDEV):
                yr = ybuf[s, pl.ds(base, 32), :]
                yi = ybuf[s, pl.ds(base + 32, 32), :]
                reim += [yr, yi]
                imre += [-yi, yr]
            right = jnp.concatenate([jnp.concatenate(reim, axis=0), jnp.concatenate(imre, axis=0)], axis=1)
            prods.append(jnp.dot(lhs, right, preferred_element_type=jnp.float32))
        off = pl.multiple_of(n * 16, 16)
        for p in range(64):
            both = jnp.concatenate([prods[0][8 * p : 8 * p + 8], prods[1][8 * p : 8 * p + 8]], axis=0)
            both = both.astype(jnp.bfloat16)
            cross[p, pl.ds(off, 16), :] = both[:, :128]
            cross[p, pl.ds(pl.multiple_of(kc + off, 16), 16), :] = both[:, 128:]

    def pairs(m, _):
        for v in range(UNROLL):
            pair(HEAD // 16 + m * UNROLL + v, v)
        return 0

    for k, ((lo, size), some) in enumerate(zip(parts, copies)):
        for copy in some:
            copy.wait()
        if k == 2:
            for copy in later:
                copy.start()
        if k:
            lax.fori_loop((lo - HEAD) // 16 // UNROLL, (lo + size - HEAD) // 16 // UNROLL, pairs, 0)
        else:
            for v in range(HEAD // 16):
                pair(v, v)
    later[0].wait()
    table = table_ref[...]
    if last:
        flags = []
        for far in range(4):
            for near in range(4):
                flags.append(xbuf[far, near * 16 : near * 16 + 4, kc * 8 - 128 :])
        flags = jnp.concatenate([f.astype(jnp.float32) for f in flags], axis=0)[:, 64:80].astype(jnp.bfloat16)
        quality = qual_ref[...].astype(jnp.float32).astype(jnp.bfloat16)
        count = jnp.dot(flags, quality, preferred_element_type=jnp.float32)
        scale[...] = 1.0 / jnp.maximum(count, 1.0)
        later[1].wait()

    def flush(n, slot):
        return pltpu.make_async_copy(stage.at[slot], out_ref.at[:, pl.ds(pl.multiple_of(n * 8, 8), 8), :], osem.at[slot])

    def save(n):
        span = pl.ds(n * 8, 8)
        return pltpu.make_async_copy(acc_ref.at[span], out_ref.at[span], osem.at[n])

    def lags(n, _):
        spots = [where_ref[n * 8 + j] for j in range(8)]
        parts = []
        for q in range(4):
            right = jnp.concatenate([cross[spots[2 * q]], cross[spots[2 * q + 1]]], axis=1)
            prod = jnp.dot(table, right, preferred_element_type=jnp.float32)
            parts += [prod[:, :128], prod[:, 128:]]
        if last:
            slot = n % 2
            parts = [(part + acc_ref[n * 8 + j]) * scale[pl.ds(spots[j], 1), :] for j, part in enumerate(parts)]

            @pl.when(n >= 2)
            def _():
                flush(n - 2, slot).wait()

            stage[slot] = pltpu.einshape("itj->tij", jnp.stack(parts, axis=0))[:NLAG]
            flush(n, slot).start()
        else:
            for j, part in enumerate(parts):
                acc_ref[n * 8 + j] = part
            save(n).start()
        return 0

    lax.fori_loop(0, 8, lags, 0)
    if last:
        flush(6, 0).wait()
        flush(7, 1).wait()
    else:
        for n in range(8):
            save(n).wait()


def correlate(first, last, kc, offset, where, ys, xs, table, qual_t, acc=None):
    smem = pl.BlockSpec(memory_space=pltpu.SMEM)
    hbm = pl.BlockSpec(memory_space=pl.ANY)
    vmem = pl.BlockSpec(memory_space=pltpu.VMEM)
    args = (where, *ys, *xs, table, qual_t)
    in_specs = [smem] + [hbm] * 9 + [vmem]
    scratch = [
        pltpu.VMEM((4, kc * 8, 128), jnp.bfloat16),
        pltpu.VMEM((4, 64, kc * 8), jnp.bfloat16),
        pltpu.VMEM((UNROLL, 128, 256), jnp.float32),
        pltpu.VMEM((64, 2 * kc, 128), jnp.bfloat16),
        pltpu.SemaphoreType.DMA((26,)),
        pltpu.VMEM((TAU, 2 * kc), jnp.bfloat16),
        pltpu.VMEM((64, TAU, 128), jnp.float32),
    ]
    if first:
        out_shape, out_specs = (64, TAU, 128), hbm
        scratch += [pltpu.SemaphoreType.DMA((8,))]
    else:
        out_shape, out_specs = (NLAG, 64, 128), hbm
        args += (acc,)
        in_specs += [hbm]
        scratch += [
            pltpu.VMEM((64, 128), jnp.float32),
            pltpu.VMEM((2, NLAG, 8, 128), jnp.float32),
            pltpu.SemaphoreType.DMA((2,)),
        ]
    return pl.pallas_call(
        functools.partial(correlate_kernel, first, last, kc, offset),
        out_shape=jax.ShapeDtypeStruct(out_shape, jnp.float32),
        in_specs=in_specs,
        out_specs=out_specs,
        scratch_shapes=scratch,
        compiler_params=pltpu.CompilerParams(vmem_limit_bytes=60 * MB),
        cost_estimate=cost(0.001),
        name="correlate_first" if first else "correlate_last",
    )(*args)


AXES = ("zhi", "core", "y", "zlo", "x")
SIZES = (2, 2, 4, 2, 4)


def permutation(move):
    out = []
    for flat in range(128):
        at = list(np.unravel_index(flat, SIZES))
        to = move(*[int(v) for v in at])
        out.append((flat, int(np.ravel_multi_index([v % n for v, n in zip(to, SIZES)], SIZES))))
    return out


def send(value, move):
    return lax.ppermute(value, AXES, permutation(move))


def sibling(zhi, core, y, zlo, x):
    return zhi, core + 1, y, zlo, x


def across(zhi, core, y, zlo, x):
    return zhi + 1, core, y, zlo, x


def ring(phase, d):
    def move(zhi, core, y, zlo, x):
        if core == phase:
            return zhi, core, y, zlo, x + d
        return zhi, core, y + d, zlo, x

    return move


def both(zhi, core, y, zlo, x):
    return zhi + 1, core + 1, y, zlo, x


def beside(zhi, core, y, zlo, x):
    return zhi, core, y, zlo + 1, x


def aside(zhi, core, y, zlo, x):
    return zhi + 1, core, y, zlo + 1, x


def on_device(traces, src_index, quality):
    samples = jnp.transpose(traces, (1, 2, 0))
    qual_t = jnp.transpose(quality, (1, 0))
    zhi, core, yy, zlo, xx = [lax.axis_index(a) for a in AXES]
    me = zhi * 2 + core
    spot = jnp.stack([me, yy * 8 + zlo * 4 + xx])
    i = jnp.arange(64, dtype=jnp.int32)
    dx, dy = (xx - i % 4) % 4, (yy - (i // 8) % 4) % 4
    dx, dy = dx % 2 * 2 + dx // 2, dy % 2 * 2 + dy // 2
    far_step, near_step = jnp.where(core == 0, dy, dx), jnp.where(core == 0, dx, dy)
    where = far_step * 16 + near_step * 4 + jnp.bitwise_xor((i // 4) % 2, zlo) * 2 + i // 32
    table = lag_table(1000)
    tables, start = [], 0
    for kc in CHUNKS:
        tables.append(jnp.asarray(np.ascontiguousarray(table[:, :, start : start + kc]).reshape(TAU, 2 * kc)))
        start += kc

    lists = [src_index] + [send(src_index, move) for move in (sibling, across, both)]
    y0, y1, y, stay, away = spectra(samples, qual_t, spot, lists)

    out = [send(stay, beside), send(away, across), send(away, aside)]
    y0, y1, y, stay, *out = lax.optimization_barrier((y0, y1, y, stay, *out))
    far0 = send(y0, across)
    held = [stay] + out
    near = send(y, sibling)
    lanes = y.shape[0]
    both_cores = [(part, j * 2, j, part) for part in range(2) for j in range(4)]
    mine, theirs = join(held, both_cores, [(8, lanes)] * 2, "join_column")
    theirs = send(theirs, sibling)
    (got,) = join((mine, theirs), [(0, 0, 0, None), (0, 8, 1, None)], [(16, lanes)], "join_cores")
    pieces = [got] + [send(got, ring(0, d)) for d in (2, 1, 3)]
    *pieces, near = lax.optimization_barrier((*pieces, near))
    far1 = send(y1, across)
    lines = split(pieces)
    xs0 = [lines[0]] + [send(lines[0], ring(1, d)) for d in (2, 1, 3)]
    *xs0, line1 = lax.optimization_barrier((*xs0, lines[1]))
    xs1 = [line1] + [send(line1, ring(1, d)) for d in (2, 1, 3)]
    acc = correlate(
        True, False, CHUNKS[0], 0, where, (y, near, far0, send(far0, sibling)), xs0, tables[0], qual_t
    )
    far1, acc, *xs1 = lax.optimization_barrier((far1, acc, *xs1))
    out = correlate(
        False, True, CHUNKS[1], CHUNKS[0], where, (y, near, far1, send(far1, sibling)), xs1, tables[1], qual_t, acc
    )
    return jnp.transpose(out, (1, 0, 2))


def solution(mesh):
    fine = Mesh(mesh.devices.reshape(2, 2, 4, 2, 4), ("zhi", "core", "y", "zlo", "x"))
    rcv = ("y", "zlo", "x")
    src = ("zhi", "core")
    return jax.shard_map(
        on_device,
        mesh=fine,
        in_specs=(P(rcv, src, None), P(src), P(rcv, None)),
        out_specs=P(src, None, rcv),
        check_vma=False,
    )
```

```python
import functools
import math

import jax
import jax.numpy as jnp
import ml_dtypes
import numpy as np
from jax import lax
from jax.experimental import pallas as pl
from jax.experimental.pallas import tpu as pltpu
from jax.sharding import Mesh, PartitionSpec as P

LAGH = 100
NLAG = 2 * LAGH + 1
TAU = 208
GRP = 8
KPAD = 1024
NGRP = KPAD // GRP
SDEV = 4
ROWS = 64
MB = 1 << 20


def start_tables(length):
    bins = np.arange(1, GRP + 1, dtype=np.float64)
    times = np.arange(length, dtype=np.float64)
    phase = 2.0 * math.pi / length * ((bins[:, None] * times[None, :]) % length)
    step = 2.0 * math.pi / length * ((GRP * times) % length)
    step = np.broadcast_to(step[None, :], phase.shape)
    return np.stack([np.cos(phase), -np.sin(phase), np.cos(step), np.sin(step)]).astype(np.float32)


def lag_table(half):
    bins = np.arange(1, half + 1, dtype=np.int64)
    lags = np.arange(-LAGH, LAGH + 1, dtype=np.int64)
    phase = 2.0 * math.pi / (2 * half) * ((lags[:, None] * bins[None, :]) % (2 * half))
    weight = np.where(bins == half, 1.0, 2.0)[None, :] / math.sqrt(half)
    out = np.zeros((TAU, 2, KPAD), np.float32)
    out[:NLAG, 0, :half] = weight * np.cos(phase)
    out[:NLAG, 1, :half] = -weight * np.sin(phase)
    return out.astype(ml_dtypes.bfloat16)


def cost(us):
    return pl.CostEstimate(flops=int(us * 1.1e9), transcendentals=0, bytes_accessed=1024)


DBLK = 25
CHUNKS = (384, 640)


def spectra_kernel(
    half, me_ref, ia, ib, ic, id_, x_hbm, start_hbm, qual_ref, y0_hbm, y1_hbm, y_hbm, stay_ref, away_ref,
    x_ref, start_ref, y_ref, state, table, spec, power, sems,
):
    ngrp = half // GRP
    length = 2 * half
    blocks = ngrp // DBLK
    me, r = me_ref[0], me_ref[1]
    load_start = pltpu.make_async_copy(start_hbm, start_ref, sems.at[0])
    load_start.start()
    load = pltpu.make_async_copy(x_hbm, x_ref, sems.at[1])
    load.start()
    load_start.wait()

    def gen(slot):
        for lo in range(0, length, 128):
            cols = slice(lo, min(lo + 128, length))
            cos, sin = state[0, :, cols], state[1, :, cols]
            rc, rs = start_ref[2, :, cols], start_ref[3, :, cols]
            for n in range(DBLK):
                table[slot, n * 16 : n * 16 + 16, cols] = jnp.concatenate([cos, sin], axis=0).astype(jnp.bfloat16)
                cos, sin = cos * rc + sin * rs, sin * rc - cos * rs
            state[0, :, cols] = cos
            state[1, :, cols] = sin

    state[0] = start_ref[0]
    state[1] = start_ref[1]
    power[...] = jnp.zeros_like(power)
    gen(0)
    load.wait()
    samples = jnp.concatenate([x_ref[g] for g in range(4)], axis=1)

    def block(b, _):
        slot = b % 2
        prod = jnp.dot(table[slot], samples, preferred_element_type=jnp.float32)
        gen(1 - slot)
        spec[pl.ds(pl.multiple_of(b * (DBLK * 16), DBLK * 16), DBLK * 16), :] = prod
        power[...] += jnp.sum((prod * prod).reshape(DBLK * 2, 8, 512), axis=0)
        return 0

    lax.fori_loop(0, blocks, block, 0)
    mean = jnp.sum(power[...], axis=0, keepdims=True) * (1.0 / half)
    level2 = 0.25 * (mean + 1e-06)
    own = [qual_ref[pl.ds(me * 4 + g, 1), :].astype(jnp.float32) for g in range(4)]

    def whiten(n):
        base = pl.multiple_of(n * 16, 16)
        reals, imags = [], []
        for g in range(4):
            cols = slice(g * 128, (g + 1) * 128)
            real = spec[pl.ds(base, 8), cols]
            imag = spec[pl.ds(base + 8, 8), cols]
            inv = lax.rsqrt(jnp.maximum(real * real + imag * imag, level2[:, cols])) * own[g]
            reals.append(real * inv)
            imags.append(imag * inv)
        value = jnp.concatenate(reals + imags, axis=0).astype(jnp.bfloat16)
        y_ref[pl.ds(pl.multiple_of(n * ROWS, ROWS), ROWS), :] = value

    first = CHUNKS[0] // GRP

    def sweep(lo, hi):
        def some(m, _):
            for v in range(5):
                whiten(lo + m * 5 + v)
            return 0

        lax.fori_loop(0, (hi - lo) // 5, some, 0)
        for n in range(hi - (hi - lo) % 5, hi):
            whiten(n)

    row = lax.broadcasted_iota(jnp.int32, (8, 128), 0)
    lane = lax.broadcasted_iota(jnp.int32, (8, 128), 1)
    hot = jnp.zeros((8, 128), jnp.float32)
    for rel, ref in enumerate((ia, ib, ic, id_)):
        for h in range(2):
            here = (row == rel * 2 + h) & (lane == ref[r + 32 * h] - r * 128)
            hot = jnp.where(here, 1.0, hot)
    hot = hot.astype(jnp.bfloat16)

    def finish(lo, hi, part_hbm, k):
        span = pl.ds(lo * ROWS, (hi - lo) * ROWS)
        copies = [
            pltpu.make_async_copy(y_ref.at[span], part_hbm, sems.at[2 * k]),
            pltpu.make_async_copy(y_ref.at[span], y_hbm.at[span], sems.at[2 * k + 1]),
        ]
        for copy in copies:
            copy.start()
        value = y_ref[lo * ROWS : hi * ROWS, :]
        picked = lax.dot_general(hot, value, (((1,), (1,)), ((), ())), preferred_element_type=jnp.float32)
        picked = picked.astype(jnp.bfloat16)
        for rel in range(4):
            out_ref = stay_ref if rel < 2 else away_ref
            out_ref[rel % 2, :, lo * ROWS : hi * ROWS] = picked[rel * 2 : rel * 2 + 2]
        return copies

    first = CHUNKS[0] // GRP
    sweep(0, first)
    copies = finish(0, first, y0_hbm, 1)
    sweep(first, ngrp)
    y_ref[ngrp * ROWS :, :] = jnp.zeros(((NGRP - ngrp) * ROWS, 128), jnp.bfloat16)
    last = (NGRP - 1) * ROWS
    y_ref[last : last + 16, :] = qual_ref[...].astype(jnp.float32).astype(jnp.bfloat16)
    copies += finish(first, NGRP, y1_hbm, 2)
    for copy in copies:
        copy.wait()


def spectra(samples, qual_t, me, lists):
    length = samples.shape[1]
    half = length // 2
    start = jnp.asarray(start_tables(length))
    vmem = pl.BlockSpec(memory_space=pltpu.VMEM)
    smem = pl.BlockSpec(memory_space=pltpu.SMEM)
    hbm = pl.BlockSpec(memory_space=pltpu.HBM)
    return pl.pallas_call(
        functools.partial(spectra_kernel, half),
        out_shape=[
            jax.ShapeDtypeStruct((CHUNKS[0] * 8, 128), jnp.bfloat16),
            jax.ShapeDtypeStruct((CHUNKS[1] * 8, 128), jnp.bfloat16),
            jax.ShapeDtypeStruct((NGRP * ROWS, 128), jnp.bfloat16),
            jax.ShapeDtypeStruct((2, 2, NGRP * ROWS), jnp.bfloat16),
            jax.ShapeDtypeStruct((2, 2, NGRP * ROWS), jnp.bfloat16),
        ],
        in_specs=[smem] * 5 + [hbm, hbm, vmem],
        out_specs=[hbm, hbm, hbm, vmem, vmem],
        scratch_shapes=[
            pltpu.VMEM((4, length, 128), jnp.bfloat16),
            pltpu.VMEM((4, 8, length), jnp.float32),
            pltpu.VMEM((NGRP * ROWS, 128), jnp.bfloat16),
            pltpu.VMEM((2, 8, length), jnp.float32),
            pltpu.VMEM((2, DBLK * 16, length), jnp.bfloat16),
            pltpu.VMEM((2 * half, 512), jnp.float32),
            pltpu.VMEM((8, 512), jnp.float32),
            pltpu.SemaphoreType.DMA((6,)),
        ],
        compiler_params=pltpu.CompilerParams(vmem_limit_bytes=63 * MB),
        cost_estimate=cost(0.001),
        name="spectra",
    )(me, *lists, samples, start, qual_t)


def join_kernel(plan, count, *refs):
    for out, row, src, at in plan:
        value = refs[src][...].reshape(-1, refs[src].shape[-1]) if at is None else refs[src][at]
        refs[count + out][row : row + value.shape[0], :] = value


def join(values, plan, shapes, name):
    vmem = pl.BlockSpec(memory_space=pltpu.VMEM)
    return pl.pallas_call(
        functools.partial(join_kernel, plan, len(values)),
        out_shape=[jax.ShapeDtypeStruct(shape, values[0].dtype) for shape in shapes],
        in_specs=[vmem] * len(values),
        out_specs=[vmem] * len(shapes),
        compiler_params=pltpu.CompilerParams(vmem_limit_bytes=16 * MB),
        cost_estimate=cost(0.001),
        name=name,
    )(*values)


def lines_kernel(pa, pb, pc, pd, *lines):
    start = 0
    for line, kc in zip(lines, CHUNKS):
        for j, piece in enumerate((pa, pb, pc, pd)):
            line[j * 16 : j * 16 + 16, :] = piece[:, start * 8 : (start + kc) * 8]
        start += kc


def split(pieces):
    vmem = pl.BlockSpec(memory_space=pltpu.VMEM)
    return pl.pallas_call(
        lines_kernel,
        out_shape=[jax.ShapeDtypeStruct((64, kc * 8), jnp.bfloat16) for kc in CHUNKS],
        in_specs=[vmem] * 4,
        out_specs=[vmem] * 2,
        compiler_params=pltpu.CompilerParams(vmem_limit_bytes=16 * MB),
        cost_estimate=cost(0.001),
        name="split",
    )(*pieces)


UNROLL = 8
HEAD = 128


def correlate_kernel(first, last, kc, offset, *refs):
    where_ref, ya, yb, yc, yd, xa, xb, xc, xd, lag_ref, qual_ref = refs[:11]
    if first:
        out_ref, ybuf, xbuf, xrow, cross, sems, table_ref, acc_ref, osem = refs[11:]
    else:
        acc_hbm, out_ref, ybuf, xbuf, xrow, cross, sems, table_ref, acc_ref, scale, stage, osem = refs[11:]
    parts = ((0, HEAD), (HEAD, 128), (HEAD + 128, kc - HEAD - 128))
    copies = []
    for k, (lo, size) in enumerate(parts):
        span = pl.ds(lo * 8, size * 8)
        some = []
        for j, ref in enumerate((ya, yc, yb, yd)):
            rows = span if j % 2 else pl.ds((offset + lo) * 8, size * 8)
            some.append(pltpu.make_async_copy(ref.at[rows], ybuf.at[j, span], sems.at[k * 8 + j]))
        for j, ref in enumerate((xa, xb, xc, xd)):
            some.append(pltpu.make_async_copy(ref.at[:, span], xbuf.at[j, :, span], sems.at[k * 8 + 4 + j]))
        copies.append(some)
        for copy in some:
            copy.start()
    later = [pltpu.make_async_copy(lag_ref, table_ref, sems.at[24])]
    if not first:
        later.append(pltpu.make_async_copy(acc_hbm, acc_ref, sems.at[25]))

    rowid = lax.broadcasted_iota(jnp.int32, (16, 256), 0) % GRP
    lane = lax.broadcasted_iota(jnp.int32, (16, 256), 1) % GRP
    keep = rowid == lane
    zero = jnp.zeros((16, 256), jnp.bfloat16)
    stay = (lax.broadcasted_iota(jnp.int32, (8, 128), 0) < 4) == (lax.broadcasted_iota(jnp.int32, (8, 128), 1) < 64)

    def pair(n, slot):
        for far in range(4):
            for near in range(4):
                tile = xbuf[far, near * 16 : near * 16 + 16, pl.ds(pl.multiple_of(n * 128, 128), 128)].astype(jnp.float32)
                for half in range(2):
                    part = tile[half * 8 : half * 8 + 8]
                    moved = pltpu.roll(pltpu.roll(part, 4, 0), 64, 1)
                    row = (far * 4 + near) * 8
                    xrow[slot, row : row + 8, half * 128 : half * 128 + 128] = jnp.where(stay, part, moved)
        prods = []
        for a in range(2):
            tiles = []
            for p in range(0, 64, 2):
                row = (p // 4) * 8 + a * 4 + p % 4
                two = jnp.concatenate(
                    [xrow[slot, pl.ds(row, 8, stride=0), :], xrow[slot, pl.ds(row + 1, 8, stride=0), :]], axis=0
                ).astype(jnp.bfloat16)
                tiles.append(jnp.where(keep, two, zero))
            lhs = jnp.concatenate(tiles, axis=0)
            base = pl.multiple_of((2 * n + a) * ROWS, ROWS)
            reim, imre = [], []
            for s in range(SDEV):
                yr = ybuf[s, pl.ds(base, 32), :]
                yi = ybuf[s, pl.ds(base + 32, 32), :]
                reim += [yr, yi]
                imre += [-yi, yr]
            right = jnp.concatenate([jnp.concatenate(reim, axis=0), jnp.concatenate(imre, axis=0)], axis=1)
            prods.append(jnp.dot(lhs, right, preferred_element_type=jnp.float32))
        off = pl.multiple_of(n * 16, 16)
        for p in range(64):
            both = jnp.concatenate([prods[0][8 * p : 8 * p + 8], prods[1][8 * p : 8 * p + 8]], axis=0)
            both = both.astype(jnp.bfloat16)
            cross[p, pl.ds(off, 16), :] = both[:, :128]
            cross[p, pl.ds(pl.multiple_of(kc + off, 16), 16), :] = both[:, 128:]

    def pairs(m, _):
        for v in range(UNROLL):
            pair(HEAD // 16 + m * UNROLL + v, v)
        return 0

    for k, ((lo, size), some) in enumerate(zip(parts, copies)):
        for copy in some:
            copy.wait()
        if k == 2:
            for copy in later:
                copy.start()
        if k:
            lax.fori_loop((lo - HEAD) // 16 // UNROLL, (lo + size - HEAD) // 16 // UNROLL, pairs, 0)
        else:
            for v in range(HEAD // 16):
                pair(v, v)
    later[0].wait()
    table = table_ref[...]
    if last:
        flags = []
        for far in range(4):
            for near in range(4):
                flags.append(xbuf[far, near * 16 : near * 16 + 4, kc * 8 - 128 :])
        flags = jnp.concatenate([f.astype(jnp.float32) for f in flags], axis=0)[:, 64:80].astype(jnp.bfloat16)
        quality = qual_ref[...].astype(jnp.float32).astype(jnp.bfloat16)
        count = jnp.dot(flags, quality, preferred_element_type=jnp.float32)
        scale[...] = 1.0 / jnp.maximum(count, 1.0)
        later[1].wait()

    def flush(n, slot):
        return pltpu.make_async_copy(stage.at[slot], out_ref.at[:, pl.ds(pl.multiple_of(n * 8, 8), 8), :], osem.at[slot])

    def save(n):
        span = pl.ds(n * 8, 8)
        return pltpu.make_async_copy(acc_ref.at[span], out_ref.at[span], osem.at[n])

    def lags(n, _):
        spots = [where_ref[n * 8 + j] for j in range(8)]
        parts = []
        for q in range(4):
            right = jnp.concatenate([cross[spots[2 * q]], cross[spots[2 * q + 1]]], axis=1)
            prod = jnp.dot(table, right, preferred_element_type=jnp.float32)
            parts += [prod[:, :128], prod[:, 128:]]
        if last:
            slot = n % 2
            parts = [(part + acc_ref[n * 8 + j]) * scale[pl.ds(spots[j], 1), :] for j, part in enumerate(parts)]

            @pl.when(n >= 2)
            def _():
                flush(n - 2, slot).wait()

            stage[slot] = pltpu.einshape("itj->tij", jnp.stack(parts, axis=0))[:NLAG]
            flush(n, slot).start()
        else:
            for j, part in enumerate(parts):
                acc_ref[n * 8 + j] = part
            save(n).start()
        return 0

    lax.fori_loop(0, 8, lags, 0)
    if last:
        flush(6, 0).wait()
        flush(7, 1).wait()
    else:
        for n in range(8):
            save(n).wait()


def correlate(first, last, kc, offset, where, ys, xs, table, qual_t, acc=None):
    smem = pl.BlockSpec(memory_space=pltpu.SMEM)
    hbm = pl.BlockSpec(memory_space=pl.ANY)
    vmem = pl.BlockSpec(memory_space=pltpu.VMEM)
    args = (where, *ys, *xs, table, qual_t)
    in_specs = [smem] + [hbm] * 9 + [vmem]
    scratch = [
        pltpu.VMEM((4, kc * 8, 128), jnp.bfloat16),
        pltpu.VMEM((4, 64, kc * 8), jnp.bfloat16),
        pltpu.VMEM((UNROLL, 128, 256), jnp.float32),
        pltpu.VMEM((64, 2 * kc, 128), jnp.bfloat16),
        pltpu.SemaphoreType.DMA((26,)),
        pltpu.VMEM((TAU, 2 * kc), jnp.bfloat16),
        pltpu.VMEM((64, TAU, 128), jnp.float32),
    ]
    if first:
        out_shape, out_specs = (64, TAU, 128), hbm
        scratch += [pltpu.SemaphoreType.DMA((8,))]
    else:
        out_shape, out_specs = (NLAG, 64, 128), hbm
        args += (acc,)
        in_specs += [hbm]
        scratch += [
            pltpu.VMEM((64, 128), jnp.float32),
            pltpu.VMEM((2, NLAG, 8, 128), jnp.float32),
            pltpu.SemaphoreType.DMA((2,)),
        ]
    return pl.pallas_call(
        functools.partial(correlate_kernel, first, last, kc, offset),
        out_shape=jax.ShapeDtypeStruct(out_shape, jnp.float32),
        in_specs=in_specs,
        out_specs=out_specs,
        scratch_shapes=scratch,
        compiler_params=pltpu.CompilerParams(vmem_limit_bytes=60 * MB),
        cost_estimate=cost(0.001),
        name="correlate_first" if first else "correlate_last",
    )(*args)


AXES = ("zhi", "core", "y", "zlo", "x")
SIZES = (2, 2, 4, 2, 4)


def permutation(move):
    out = []
    for flat in range(128):
        at = list(np.unravel_index(flat, SIZES))
        to = move(*[int(v) for v in at])
        out.append((flat, int(np.ravel_multi_index([v % n for v, n in zip(to, SIZES)], SIZES))))
    return out


def send(value, move):
    return lax.ppermute(value, AXES, permutation(move))


def sibling(zhi, core, y, zlo, x):
    return zhi, core + 1, y, zlo, x


def across(zhi, core, y, zlo, x):
    return zhi + 1, core, y, zlo, x


def ring(phase, d):
    def move(zhi, core, y, zlo, x):
        if core == phase:
            return zhi, core, y, zlo, x + d
        return zhi, core, y + d, zlo, x

    return move


def both(zhi, core, y, zlo, x):
    return zhi + 1, core + 1, y, zlo, x


def beside(zhi, core, y, zlo, x):
    return zhi, core, y, zlo + 1, x


def aside(zhi, core, y, zlo, x):
    return zhi + 1, core, y, zlo + 1, x


def on_device(traces, src_index, quality):
    samples = jnp.transpose(traces, (1, 2, 0))
    qual_t = jnp.transpose(quality, (1, 0))
    zhi, core, yy, zlo, xx = [lax.axis_index(a) for a in AXES]
    me = zhi * 2 + core
    spot = jnp.stack([me, yy * 8 + zlo * 4 + xx])
    i = jnp.arange(64, dtype=jnp.int32)
    dx, dy = (xx - i % 4) % 4, (yy - (i // 8) % 4) % 4
    dx, dy = dx % 2 * 2 + dx // 2, dy % 2 * 2 + dy // 2
    far_step, near_step = jnp.where(core == 0, dy, dx), jnp.where(core == 0, dx, dy)
    where = far_step * 16 + near_step * 4 + jnp.bitwise_xor((i // 4) % 2, zlo) * 2 + i // 32
    table = lag_table(1000)
    tables, start = [], 0
    for kc in CHUNKS:
        tables.append(jnp.asarray(np.ascontiguousarray(table[:, :, start : start + kc]).reshape(TAU, 2 * kc)))
        start += kc

    lists = [src_index] + [send(src_index, move) for move in (sibling, across, both)]
    y0, y1, y, stay, away = spectra(samples, qual_t, spot, lists)

    out = [send(stay, beside), send(away, across), send(away, aside)]
    y0, y1, y, stay, *out = lax.optimization_barrier((y0, y1, y, stay, *out))
    far0 = send(y0, across)
    held = [stay] + out
    near = send(y, sibling)
    lanes = y.shape[0]
    both_cores = [(part, j * 2, j, part) for part in range(2) for j in range(4)]
    mine, theirs = join(held, both_cores, [(8, lanes)] * 2, "join_column")
    theirs = send(theirs, sibling)
    (got,) = join((mine, theirs), [(0, 0, 0, None), (0, 8, 1, None)], [(16, lanes)], "join_cores")
    pieces = [got] + [send(got, ring(0, d)) for d in (2, 1, 3)]
    *pieces, near = lax.optimization_barrier((*pieces, near))
    far1 = send(y1, across)
    lines = split(pieces)
    xs0 = [lines[0]] + [send(lines[0], ring(1, d)) for d in (2, 1, 3)]
    *xs0, line1 = lax.optimization_barrier((*xs0, lines[1]))
    xs1 = [line1] + [send(line1, ring(1, d)) for d in (2, 1, 3)]
    acc = correlate(
        True, False, CHUNKS[0], 0, where, (y, near, far0, send(far0, sibling)), xs0, tables[0], qual_t
    )
    far1, acc, *xs1 = lax.optimization_barrier((far1, acc, *xs1))
    out = correlate(
        False, True, CHUNKS[1], CHUNKS[0], where, (y, near, far1, send(far1, sibling)), xs1, tables[1], qual_t, acc
    )
    return jnp.transpose(out, (1, 0, 2))


def solution(mesh):
    fine = Mesh(mesh.devices.reshape(2, 2, 4, 2, 4), ("zhi", "core", "y", "zlo", "x"))
    rcv = ("y", "zlo", "x")
    src = ("zhi", "core")
    return jax.shard_map(
        on_device,
        mesh=fine,
        in_specs=(P(rcv, src, None), P(src), P(rcv, None)),
        out_specs=P(src, None, rcv),
        check_vma=False,
    )
```
